512 devices in a mesh: gx: 32 (over y, z_lo), gy: 16 (over x, z_hi, core).
Axes of the slice: x: 4, y: 4, z: 16 (z_hi: 2, z_lo: 8; z = z_hi * 8 + z_lo), core: 2. Of those that a mesh axis runs over, the one named last changes fastest.
Arguments:
- latent: bfloat16 [128, 2048, 128], P('gx', 'gy'), may hold values from -6 to 6
- corr_kernel: bfloat16 [128, 128], replicated, may hold values from -0.5 to 0.5
- first_conv_weight: bfloat16 [3, 3, 128, 128], replicated, may hold values from -0.1875 to 0.1875
- first_conv_bias: float32 [128], replicated, may hold values from -3 to 3
- second_conv_weight: bfloat16 [3, 3, 128, 128], replicated, may hold values from -0.1875 to 0.1875
- second_conv_bias: float32 [128], replicated, may hold values from -3 to 3
- cotangent: bfloat16 [128, 2048, 128], P('gx', 'gy'), may hold values from -0.01171875 to 0.01171875
Outputs:
- prediction: bfloat16 [128, 2048, 128], P('gx', 'gy')
- conv1_weight_grad: float32 [3, 3, 128, 128], replicated
- conv1_bias_grad: float32 [128], replicated
- conv2_weight_grad: float32 [3, 3, 128, 128], replicated
- conv2_bias_grad: float32 [128], replicated
- kernel_grad: float32 [128, 128], replicated
The draws below stay inside these ranges and needn't reach their ends.
All inputs are finite; a program needn't handle non-finite values.
Results may differ from the reference program's by a relative error of at most 0.0095.
Values may be sent and summed in bfloat16 or wider, within the bound.
No kernel may reach another device: no remote copies, remote signals or barrier semaphores. Data moves between devices by JAX's collectives and lax.ppermute only.
A program may use at most 64 MiB of HBM per device.

```python
import jax
import jax.numpy as jnp
from jax import lax

C = 128
DILATION_FIRST = 1
DILATION_SECOND = 2
NX = 128
NY = 2048


def steps_of(own_key, dims, split, low, high):
    def one(axis_at, shards_of):
        heights = jax.random.uniform(jax.random.fold_in(jax.random.fold_in(own_key, 6), axis_at), (shards_of,), jnp.float32, low / len(split), high / len(split))
        return jnp.repeat(jnp.exp(heights), dims[axis_at] // shards_of).reshape((-1,) + (1,) * (len(dims) - axis_at - 1))

    factor_of = one(*split[0])
    for cut in split[1:]:
        factor_of = factor_of * one(*cut)
    return factor_of


def bell_draw(rng, shape, deviation, limit, cuts=(), kind=jnp.bfloat16):
    factor_of = steps_of(rng, shape, cuts, -0.22, 0.18) if cuts else 1.0
    entries = jax.random.normal(rng, shape, jnp.float32) * deviation * factor_of
    return jnp.minimum(jnp.maximum(entries, -limit), limit).astype(kind)


def setup_inputs(seed: int = 0) -> dict:
    splits = jax.random.split(jax.random.key(seed), 8)
    latent = bell_draw(splits[0], (NX, NY, C), 1.0, 6.0, ((0, 32), (1, 16)))
    corr_kernel = bell_draw(splits[1], (NX, C), NX ** -0.5, 0.5)
    first_conv_weight = bell_draw(splits[2], (3, 3, C, C), (9 * C) ** -0.5, 0.1875)
    first_conv_bias = bell_draw(splits[3], (C,), 0.5, 3.0, (), jnp.float32)
    second_conv_weight = bell_draw(splits[4], (3, 3, C, C), (9 * C) ** -0.5, 0.1875)
    second_conv_bias = bell_draw(splits[5], (C,), 0.5, 3.0, (), jnp.float32)
    cotangent = bell_draw(splits[6], (NX, NY, C), (1.0 / (NX * NY) ** 0.5), 0.01171875, ((0, 32), (1, 16)))
    return dict(latent=latent, corr_kernel=corr_kernel, first_conv_weight=first_conv_weight, first_conv_bias=first_conv_bias, second_conv_weight=second_conv_weight, second_conv_bias=second_conv_bias, cotangent=cotangent)


def silu_slope(preact):
    logistic = jax.nn.sigmoid(preact)
    return logistic * (1.0 + preact * (1.0 - logistic))


def correlate_rows(latent, corr_kernel):
    blocks_out = []
    for block_start in range(0, C, 16):
        field = latent[:, :, block_start:block_start + 16].astype(jnp.float32)
        kernel_part = corr_kernel[:, block_start:block_start + 16].astype(jnp.float32)
        spectrum = jnp.fft.fft(field, axis=0) * jnp.conj(jnp.fft.fft(kernel_part, axis=0))[:, None, :]
        blocks_out.append(jnp.real(jnp.fft.ifft(spectrum, axis=0)))
    return jnp.concatenate(blocks_out, axis=-1)


def kernel_gradient(mixed_gradient, latent):
    blocks_out = []
    for block_start in range(0, C, 16):
        grad_part = jnp.fft.fft(mixed_gradient[:, :, block_start:block_start + 16].astype(jnp.float32), axis=0)
        field_part = jnp.fft.fft(latent[:, :, block_start:block_start + 16].astype(jnp.float32), axis=0)
        cross = jnp.sum(jnp.conj(grad_part) * field_part, axis=1)
        blocks_out.append(jnp.real(jnp.fft.ifft(cross, axis=0)))
    return jnp.concatenate(blocks_out, axis=-1)


def dilated_conv_apply(field, weight, bias_vec, dilation):
    running = jnp.zeros((NX * NY, C), jnp.float32) + bias_vec
    for row_off in (-1, 0, 1):
        for col_off in (-1, 0, 1):
            moved = jnp.roll(field, (-row_off * dilation, -col_off * dilation), axis=(0, 1))
            running = running + jnp.dot(moved.reshape(-1, C), weight[row_off + 1, col_off + 1], preferred_element_type=jnp.float32)
    return running.reshape(NX, NY, C)


def dilated_conv_weight_gradient(field, slope, dilation):
    flat_slope = slope.reshape(-1, C)
    rows_out = []
    for row_off in (-1, 0, 1):
        cols_out = []
        for col_off in (-1, 0, 1):
            moved = jnp.roll(field, (-row_off * dilation, -col_off * dilation), axis=(0, 1)).reshape(-1, C)
            cols_out.append(lax.dot_general(moved, flat_slope, (((0,), (0,)), ((), ())), preferred_element_type=jnp.float32))
        rows_out.append(jnp.stack(cols_out))
    return jnp.stack(rows_out)


def dilated_conv_adjoint(slope, weight, dilation):
    running = jnp.zeros((NX * NY, C), jnp.float32)
    for row_off in (-1, 0, 1):
        for col_off in (-1, 0, 1):
            moved = jnp.roll(slope, (row_off * dilation, col_off * dilation), axis=(0, 1))
            running = running + jnp.dot(moved.reshape(-1, C), weight[row_off + 1, col_off + 1].T, preferred_element_type=jnp.float32)
    return running.reshape(NX, NY, C)


def reference(latent, corr_kernel, first_conv_weight, first_conv_bias, second_conv_weight, second_conv_bias, cotangent):
    mixed_field = (latent.astype(jnp.float32) + correlate_rows(latent, corr_kernel)).astype(jnp.bfloat16)
    first_preactivation = dilated_conv_apply(mixed_field, first_conv_weight, first_conv_bias, DILATION_FIRST)
    hidden_activation = (mixed_field.astype(jnp.float32) + jax.nn.silu(first_preactivation)).astype(jnp.bfloat16)
    second_preactivation = dilated_conv_apply(hidden_activation, second_conv_weight, second_conv_bias, DILATION_SECOND)
    prediction = (hidden_activation.astype(jnp.float32) + jax.nn.silu(second_preactivation)).astype(jnp.bfloat16)
    incoming_gradient = cotangent.astype(jnp.float32)
    second_activation_slope = (incoming_gradient * silu_slope(second_preactivation)).astype(jnp.bfloat16)
    second_weight_matrix = dilated_conv_weight_gradient(hidden_activation, second_activation_slope, DILATION_SECOND)
    bias_two = jnp.sum(second_activation_slope.astype(jnp.float32), axis=(0, 1))
    hidden_gradient = incoming_gradient + dilated_conv_adjoint(second_activation_slope, second_conv_weight, DILATION_SECOND)
    first_activation_slope = (hidden_gradient * silu_slope(first_preactivation)).astype(jnp.bfloat16)
    first_weight_matrix = dilated_conv_weight_gradient(mixed_field, first_activation_slope, DILATION_FIRST)
    bias_one = jnp.sum(first_activation_slope.astype(jnp.float32), axis=(0, 1))
    mixed_gradient = (hidden_gradient + dilated_conv_adjoint(first_activation_slope, first_conv_weight, DILATION_FIRST)).astype(jnp.bfloat16)
    kernel_grad = kernel_gradient(mixed_gradient, latent)
    return (prediction, first_weight_matrix, bias_one, second_weight_matrix, bias_two, kernel_grad)
```

```python
import jax
import jax.numpy as jnp
import numpy as np
from jax import lax
from jax.sharding import Mesh, PartitionSpec as P

ROWS_AXES = ("y", "zl")
COLS_AXES = ("x", "zh", "c")
PLANE_AXES = ("y", "x", "c")
DEPTH_AXES = ("zl", "zh")
N_ROWS = 128
OWN = 4
HALO_LAT = 5
HALO_COT = 2
GRAD_ROWS = 2560


def real_transform(order):
    freq = np.arange(64)
    angle = 2.0 * np.pi * ((freq[:, None] * order[None, :]) % N_ROWS) / N_ROWS
    sines = np.sin(angle)
    sines[0] = np.cos(np.pi * order)
    return np.concatenate([np.cos(angle), sines])


def split_two(table):
    high = table.astype(jnp.bfloat16)
    low = (table - high.astype(np.float64)).astype(jnp.bfloat16)
    return high, low


def silu_slope(preact):
    logistic = jax.nn.sigmoid(preact)
    return logistic * (1.0 + preact * (1.0 - logistic))


def shift_rows(x, step):
    width, _, channels = x.shape
    x = x.reshape(width, 4, 32, channels)
    if step > 0:
        out = jnp.concatenate([x[:, step:], jnp.roll(x[:, :step], -1, axis=2)], axis=1)
    elif step < 0:
        out = jnp.concatenate([jnp.roll(x[:, step:], 1, axis=2), x[:, :step]], axis=1)
    else:
        out = x
    return out.reshape(width, 128, channels)


def taps(x, dilation, sign):
    rows = jnp.concatenate([shift_rows(x, sign * p * dilation) for p in (-1, 0, 1)], axis=-1)
    width = x.shape[0]
    kept = width - 2 * dilation
    cols = [rows[dilation + sign * q * dilation :][:kept] for q in (-1, 0, 1)]
    return jnp.concatenate(cols, axis=-1)


def matmul(a, b):
    return jnp.dot(a, b, preferred_element_type=jnp.float32)


def spectrum(table_hi, table_lo, field):
    def one(table):
        return jnp.einsum("fr,jrc->jfc", table, field, preferred_element_type=jnp.float32)

    return one(table_hi) + one(table_lo)


def cross(first, second):
    fc, fs = first[..., :64, :], first[..., 64:, :]
    sc, ss = second[..., :64, :], second[..., 64:, :]
    real_row = lax.broadcasted_iota(jnp.int32, (64, 1), 0) == 0
    out_c = sc * fc + jnp.where(real_row, 0.0, ss * fs)
    out_s = jnp.where(real_row, ss * fs, ss * fc - sc * fs)
    return jnp.concatenate([out_c, out_s], axis=-2)


def per_device(latent, corr_kernel, w1, b1, w2, b2, cotangent):
    bf, f4 = jnp.bfloat16, jnp.float32
    row_count, col_count, channels = latent.shape
    n_rows_dev = lax.axis_size(ROWS_AXES)
    n_cols_dev = lax.axis_size(COLS_AXES)
    up = [(i, (i + 1) % n_cols_dev) for i in range(n_cols_dev)]
    down = [(j, i) for i, j in up]
    edge_hi = jnp.concatenate([latent[:, -HALO_LAT:], cotangent[:, -HALO_COT:]], axis=1)
    edge_lo = jnp.concatenate([latent[:, :HALO_LAT], cotangent[:, :HALO_COT]], axis=1)
    left = lax.ppermute(edge_hi, COLS_AXES, up)
    right = lax.ppermute(edge_lo, COLS_AXES, down)
    pad = jnp.zeros((row_count, 2, channels), bf)
    lat_ext = jnp.concatenate([left[:, :HALO_LAT], latent, right[:, :HALO_LAT], pad], axis=1)
    cot_ext = jnp.concatenate([left[:, HALO_LAT:], cotangent, right[:, HALO_LAT:]], axis=1)
    lat_blocks = lat_ext.transpose(1, 0, 2).reshape(-1, 4, row_count, channels)
    cot_blocks = cot_ext.transpose(1, 0, 2).reshape(-1, 4, row_count, channels)
    n = n_rows_dev
    send = jnp.concatenate(
        [lat_blocks[0:n], lat_blocks[1 : n + 1], lat_blocks[2 : n + 2], lat_blocks[3 : n + 3, :2],
         cot_blocks[0:n], cot_blocks[1 : n + 1]],
        axis=1,
    )
    got = lax.all_to_all(send, ROWS_AXES, 0, 0, tiled=True)
    cells = got.transpose(1, 2, 0, 3).reshape(22, N_ROWS, channels)
    lat, cot = cells[:14], cells[14:].astype(f4)

    place = np.arange(N_ROWS)
    order = 4 * (place % 32) + place // 32
    t_hi, t_lo = split_two(real_transform(order))
    n_hi, n_lo = split_two(real_transform(place))
    weight = np.full((N_ROWS, 1), 2.0 / N_ROWS)
    weight[0] = weight[64] = 1.0 / N_ROWS
    inv_perm = jnp.asarray((real_transform(order) * weight).T, f4)
    inv_nat = jnp.asarray((real_transform(place) * weight).T, f4)

    lat_spec = spectrum(t_hi, t_lo, lat)
    ker_spec = spectrum(n_hi, n_lo, corr_kernel[None])[0]
    prod = cross(ker_spec[None], lat_spec)
    correlated = jnp.einsum("rf,jfc->jrc", inv_perm, prod, precision=lax.Precision.HIGHEST, preferred_element_type=f4)
    mixed = (lat.astype(f4) + correlated).astype(bf)

    w1_flat = w1.transpose(1, 0, 2, 3).reshape(9 * channels, channels)
    w2_flat = w2.transpose(1, 0, 2, 3).reshape(9 * channels, channels)
    w1_back = w1.transpose(1, 0, 3, 2).reshape(9 * channels, channels)
    w2_back = w2.transpose(1, 0, 3, 2).reshape(9 * channels, channels)

    mixed_taps = taps(mixed, 1, 1)
    pre1 = matmul(mixed_taps, w1_flat) + b1
    hidden = (mixed[1:13].astype(f4) + jax.nn.silu(pre1)).astype(bf)
    hidden_taps = taps(hidden, 2, 1)
    pre2 = matmul(hidden_taps, w2_flat) + b2
    prediction = (hidden[4:8].astype(f4) + jax.nn.silu(pre2[2:6])).astype(bf)
    pred_send = prediction.reshape(OWN, 4, n, channels).transpose(2, 0, 1, 3)
    pred_got = lax.all_to_all(pred_send, ROWS_AXES, 0, 0, tiled=True)
    pred_out = pred_got.transpose(2, 0, 1, 3).reshape(row_count, col_count, channels)

    slope2 = (cot * silu_slope(pre2)).astype(bf)
    own2 = slope2[2:6].reshape(-1, channels)
    dot_t = lambda a, b: lax.dot_general(a, b, (((0,), (0,)), ((), ())), preferred_element_type=f4)
    dw2 = dot_t(hidden_taps[2:6].reshape(-1, 9 * channels), own2)
    db2 = jnp.sum(own2.astype(f4), axis=0)
    grad_hidden = cot[2:6] + matmul(taps(slope2, 2, -1), w2_back)
    slope1 = (grad_hidden * silu_slope(pre1[4:8])).astype(bf)
    own1 = slope1.reshape(-1, channels)
    dw1 = dot_t(mixed_taps[4:8].reshape(-1, 9 * channels), own1)
    db1 = jnp.sum(own1.astype(f4), axis=0)
    spread = matmul(taps(jnp.pad(slope1, ((2, 2), (0, 0), (0, 0))), 1, -1), w1_back)
    grad_mixed = (spread + jnp.pad(grad_hidden, ((1, 1), (0, 0), (0, 0)))).astype(bf)
    grad_spec = spectrum(t_hi, t_lo, grad_mixed)
    both = jnp.sum(cross(grad_spec, lat_spec[4:10]), axis=0)
    dk = jnp.dot(inv_nat, both, precision=lax.Precision.HIGHEST, preferred_element_type=f4)

    biases = jnp.stack([db1, db2])
    high = biases.astype(bf)
    low = (biases - high.astype(f4)).astype(bf)
    grads = jnp.concatenate(
        [dw1.astype(bf), dw2.astype(bf), dk.astype(bf), high, low, jnp.zeros((GRAD_ROWS - 2436, channels), bf)]
    )
    n_plane, n_depth = lax.axis_size(PLANE_AXES), lax.axis_size(DEPTH_AXES)
    share = GRAD_ROWS // n_plane
    part = lax.all_to_all(grads.reshape(n_plane, share, channels), PLANE_AXES, 0, 0, tiled=True)
    part = jnp.sum(part.astype(f4), axis=0).astype(bf)
    part = lax.all_to_all(jnp.broadcast_to(part, (n_depth, share, channels)), DEPTH_AXES, 0, 0, tiled=True)
    part = jnp.sum(part.astype(f4), axis=0).astype(bf)
    whole = lax.all_to_all(jnp.broadcast_to(part, (n_plane, share, channels)), PLANE_AXES, 0, 0, tiled=True)
    whole = whole.reshape(GRAD_ROWS, channels).astype(f4)
    dw1, dw2 = (whole[a : a + 1152].reshape(3, 3, channels, channels).transpose(1, 0, 2, 3) for a in (0, 1152))
    return pred_out, dw1, whole[2432] + whole[2434], dw2, whole[2433] + whole[2435], whole[2304:2432]


def solution(mesh):
    axes = ROWS_AXES + COLS_AXES
    split = Mesh(mesh.devices.reshape(4, 8, 4, 2, 2), axes)
    grid = P(ROWS_AXES, COLS_AXES, None)
    return jax.shard_map(
        per_device, mesh=split, in_specs=(grid, P(), P(), P(), P(), P(), grid),
        out_specs=(grid, P(), P(), P(), P(), P()), check_vma=False,
    )
```

```python
import jax
import jax.numpy as jnp
import numpy as np
from jax import lax
from jax.experimental import pallas as pl
from jax.experimental.pallas import tpu as pltpu
from jax.sharding import Mesh, PartitionSpec as P

ROWS_AXES = ("y", "zl")
COLS_AXES = ("x", "zh", "c")
PLANE_AXES = ("y", "x", "c")
DEPTH_AXES = ("zl", "zh")
SIZES = {"y": 4, "zl": 8, "x": 4, "zh": 2, "c": 2}
N_ROWS = 128
CH = 128
PEERS = 32
GRAD_ROWS = 2560
BF, F4 = jnp.bfloat16, jnp.float32
VMEM = pl.BlockSpec(memory_space=pltpu.VMEM)


def real_transform(order):
    freq = np.arange(64)
    angle = 2.0 * np.pi * ((freq[:, None] * order[None, :]) % N_ROWS) / N_ROWS
    sines = np.sin(angle)
    sines[0] = np.cos(np.pi * order)
    return np.concatenate([np.cos(angle), sines])


def split_two(table):
    high = table.astype(jnp.bfloat16)
    low = (table - high.astype(np.float64)).astype(jnp.bfloat16)
    return high, low


def tables():
    place = np.arange(N_ROWS)
    order = 4 * (place % 32) + place // 32
    weight = np.full((N_ROWS, 1), 2.0 / N_ROWS)
    weight[0] = weight[64] = 1.0 / N_ROWS
    made = []
    for rows in (order, place):
        made.append(np.concatenate(split_two(real_transform(rows)), axis=1))
        high, low = split_two((real_transform(rows) * weight).T)
        made.append(np.concatenate([high, high, low], axis=1))
    return made


def window_of(y, zl, flip):
    snake = zl * 4 + jnp.where(zl % 2 == 0, y, 3 - y)
    return jnp.where(flip, 31 - snake, snake)


def flipped(zh, c):
    return zh == c


def device_ring():
    ring = []
    for x in range(4):
        for zh in range(2):
            for c in range(2):
                block = [0] * 32
                for y in range(4):
                    for zl in range(8):
                        snake = zl * 4 + (y if zl % 2 == 0 else 3 - y)
                        block[31 - snake if flipped(zh, c) else snake] = (((y * 8 + zl) * 4 + x) * 2 + zh) * 2 + c
                ring += block
    return ring


def dot(a, b):
    return jnp.dot(a, b, preferred_element_type=F4)


def dot_t(a, b):
    return lax.dot_general(a, b, (((0,), (0,)), ((), ())), preferred_element_type=F4)


def turned(x, step):
    blocks = [x[32 * i : 32 * i + 32] for i in range(4)]
    if step > 0:
        moved = [pltpu.roll(b, 31, axis=0) for b in blocks[:step]]
        return jnp.concatenate(blocks[step:] + moved, axis=0)
    if step < 0:
        moved = [pltpu.roll(b, 1, axis=0) for b in blocks[step:]]
        return jnp.concatenate(moved + blocks[:step], axis=0)
    return x


def put_turned(ref, col, x, steps):
    for i, step in enumerate(steps):
        ref[col, :, i * CH : (i + 1) * CH] = turned(x, step).astype(BF)


def cross(first, second):
    fc, fs = first[:64], first[64:]
    sc, ss = second[:64], second[64:]
    real_row = lax.broadcasted_iota(jnp.int32, sc.shape, 0) == 0
    out_c = sc * fc + jnp.where(real_row, 0.0, ss * fs)
    out_s = jnp.where(real_row, ss * fs, ss * fc - sc * fs)
    return jnp.concatenate([out_c, out_s], axis=0)


def three_parts(x):
    high = x.astype(BF)
    low = (x - high.astype(F4)).astype(BF)
    return jnp.concatenate([high, low, high], axis=0)


def send_kernel(lat, cot, out, wide, packed):
    y, zl, zh, c = (lax.axis_index(a) for a in ("y", "zl", "zh", "c"))
    flip = flipped(zh, c)
    for t, ref in enumerate((lat, cot)):
        wide[t * 512 : t * 512 + 512, :] = ref[...].reshape(512, CH).astype(F4)
    for k in range(PEERS):
        start = pl.multiple_of(4 * window_of(k // 8, jnp.int32(k % 8), flip), 4)
        for t in range(2):
            for rr in range(4):
                piece = wide[pl.ds(t * 512 + rr * 128 + start, 4), :]
                packed[pl.ds(k * 32 + t * 16 + rr, 4, stride=4), :] = piece
    out[...] = packed[...].astype(BF).reshape(PEERS, 32, CH)


def column(ref, start, stride):
    return jnp.concatenate([ref[pl.ds(start + rr, 32, stride=stride), :] for rr in range(4)], axis=0)


def forward_kernel(far_left, left, own, right, far_right, ker, w1, b1, w2, b2, fwd, inv, fwd_nat,
                   pred, spec, m3, h3, rise1, slope2, cot_own,
                   gl, go, gr, gl2, gr2, latf, xw, parts, cots, hid, placed):
    for ref, wide in ((left, gl), (own, go), (right, gr), (far_left, gl2), (far_right, gr2)):
        wide[...] = ref[...].reshape(wide.shape).astype(F4)
    lat_from = ([(gl2, 4, 8)] + [(gl, 4 * j, 32) for j in range(4)] + [(go, 4 * j, 32) for j in range(4)]
                + [(gr, 4 * j, 32) for j in range(4)] + [(gr2, 0, 8)])
    for j, (ref, start, stride) in enumerate(lat_from):
        x = column(ref, start, stride)
        latf[j] = x
        xb = x.astype(BF)
        xw[0:128, j * CH : (j + 1) * CH] = xb
        xw[128:256, j * CH : (j + 1) * CH] = xb
    cot_from = [(gl, 24), (gl, 28)] + [(go, 16 + 4 * j) for j in range(4)] + [(gr, 16), (gr, 20)]
    for u, (ref, start) in enumerate(cot_from):
        cots[u] = column(ref, start, 32)
    cot_own[...] = cots[2:6]
    ker_two = jnp.concatenate([ker[...], ker[...]], axis=0)
    ker_spec = dot(fwd_nat[...], ker_two)
    for j in range(0, 14, 2):
        lanes = slice(j * CH, (j + 2) * CH)
        s = dot(fwd[...], xw[:, lanes])
        if 4 <= j < 10:
            spec[:, (j - 4) * CH : (j - 2) * CH] = s
        for i in range(2):
            part = s[:, i * CH : (i + 1) * CH]
            parts[:, i * CH : (i + 1) * CH] = three_parts(cross(ker_spec, part))
        corr = dot(inv[...], parts[...])
        for i in range(2):
            mixed = (latf[j + i] + corr[:, i * CH : (i + 1) * CH]).astype(BF).astype(F4)
            latf[j + i] = mixed
            put_turned(m3, j + i, mixed, (-1, 0, 1))
    for j in range(0, 12, 4):
        v = b1[...]
        for q in range(3):
            v = v + dot(m3[j + q : j + q + 4].reshape(512, 384), w1[q])
        g = jax.nn.sigmoid(v)
        if j == 4:
            rise1[...] = (g * (1.0 + v * (1.0 - g))).reshape(4, N_ROWS, CH)
        vg = v * g
        for i in range(4):
            h = (latf[j + i + 1] + vg[i * 128 : i * 128 + 128]).astype(BF).astype(F4)
            hid[j + i] = h
            put_turned(h3, j + i, h, (-2, 0, 2))
    for j in range(0, 8, 4):
        v = b2[...]
        for q in range(3):
            v = v + dot(h3[j + 2 * q : j + 2 * q + 4].reshape(512, 384), w2[q])
        g = jax.nn.sigmoid(v)
        vg = v * g
        rise = g * (1.0 + v * (1.0 - g))
        for i in range(4):
            u = j + i
            slope2[u] = (cots[u] * rise[i * 128 : i * 128 + 128]).astype(BF)
            if 2 <= u < 6:
                p = hid[u + 2] + vg[i * 128 : i * 128 + 128]
                for rr in range(4):
                    placed[pl.ds((u - 2) * 4 + rr, 32, stride=16), :] = p[rr * 32 : rr * 32 + 32]
    pred[...] = placed[...].astype(BF).reshape(PEERS, 16, CH)


def backward_kernel(spec, m3, h3, rise1, slope2, cot_own, w1b, w2b, fwd, inv_nat, out, s3, z3, gm):
    own2 = slope2[2:6].reshape(512, CH)
    for q in range(3):
        d = dot_t(h3[2 + 2 * q : 6 + 2 * q].reshape(512, 384), own2)
        for p in range(3):
            out[1152 + (p * 3 + q) * 128 : 1280 + (p * 3 + q) * 128, :] = d[p * 128 : p * 128 + 128].astype(BF)
    for u in range(8):
        put_turned(s3, u, slope2[u].astype(F4), (2, 0, -2))
    gh = cot_own[...].reshape(512, CH)
    for q in range(3):
        gh = gh + dot(s3[4 - 2 * q : 8 - 2 * q].reshape(512, 384), w2b[q])
    slope1 = (gh * rise1[...].reshape(512, CH)).astype(BF)
    slope1_wide = slope1.astype(F4)
    for i in range(4):
        put_turned(z3, i, slope1_wide[i * 128 : i * 128 + 128], (1, 0, -1))
    gm[0] = jnp.zeros((N_ROWS, CH), F4)
    gm[5] = jnp.zeros((N_ROWS, CH), F4)
    gm[1:5] = gh.reshape(4, N_ROWS, CH)
    for q in range(3):
        gm[q : q + 4] += dot(z3[...].reshape(512, 384), w1b[q]).reshape(4, N_ROWS, CH)
    for q in range(3):
        d = dot_t(m3[4 + q : 8 + q].reshape(512, 384), slope1)
        for p in range(3):
            out[(p * 3 + q) * 128 : (p * 3 + q) * 128 + 128, :] = d[p * 128 : p * 128 + 128].astype(BF)
    both = jnp.zeros((N_ROWS, CH), F4)
    for j in range(0, 6, 2):
        two = jnp.concatenate([gm[j], gm[j + 1]], axis=1).astype(BF)
        s = dot(fwd[...], jnp.concatenate([two, two], axis=0))
        for i in range(2):
            both = both + cross(s[:, i * CH : (i + 1) * CH], spec[:, (j + i) * CH : (j + i + 1) * CH])
    dk = dot(inv_nat[...], three_parts(both))
    out[2304:2432, :] = dk.astype(BF)
    db1 = jnp.sum(slope1_wide, axis=0, keepdims=True)
    db2 = jnp.sum(own2.astype(F4), axis=0, keepdims=True)
    rows = []
    for b in (db1, db2):
        high = b.astype(BF).astype(F4)
        rows += [high, b - high]
    tail = jnp.concatenate(rows + [jnp.zeros((GRAD_ROWS - 2436, CH), F4)], axis=0)
    out[2432:GRAD_ROWS, :] = tail.astype(BF)


def call(kernel, outs, scratch, flops, *args):
    return pl.pallas_call(
        kernel,
        out_shape=[jax.ShapeDtypeStruct(s, d) for s, d in outs],
        in_specs=[VMEM] * len(args),
        out_specs=[VMEM] * len(outs),
        scratch_shapes=[pltpu.VMEM(s, d) for s, d in scratch],
        compiler_params=pltpu.CompilerParams(vmem_limit_bytes=40 << 20),
        cost_estimate=pl.CostEstimate(flops=flops, bytes_accessed=4 << 20, transcendentals=0),
    )(*args)


def forward(far_left, left, own, right, far_right, ker, w1, b1, w2, b2):
    fwd, inv, fwd_nat, _ = (jnp.asarray(t, BF) for t in tables())
    w1q = w1.transpose(1, 0, 2, 3).reshape(3, 384, CH)
    w2q = w2.transpose(1, 0, 2, 3).reshape(3, 384, CH)
    outs = [((PEERS, 16, CH), BF), ((128, 6 * CH), F4), ((14, 128, 384), BF), ((12, 128, 384), BF),
            ((4, 128, CH), F4), ((8, 128, CH), BF), ((4, 128, CH), F4)]
    scratch = [((1024, CH), F4)] * 3 + [((256, CH), F4)] * 2 + [
        ((14, 128, CH), F4), ((256, 14 * CH), BF), ((384, 2 * CH), BF), ((8, 128, CH), F4), ((12, 128, CH), F4),
        ((512, CH), F4)]
    return call(forward_kernel, outs, scratch, 1 << 30, far_left, left, own, right, far_right, ker,
                w1q, b1.reshape(1, CH), w2q, b2.reshape(1, CH), fwd, inv, fwd_nat)


def backward(w1, w2, spec, m3, h3, rise1, slope2, cot_own):
    fwd, _, _, inv_nat = (jnp.asarray(t, BF) for t in tables())
    w1b = w1.transpose(1, 0, 3, 2).reshape(3, 384, CH)
    w2b = w2.transpose(1, 0, 3, 2).reshape(3, 384, CH)
    outs = [((GRAD_ROWS, CH), BF)]
    scratch = [((8, 128, 384), BF), ((4, 128, 384), BF), ((6, 128, CH), F4)]
    return call(backward_kernel, outs, scratch, 1 << 31, spec, m3, h3, rise1, slope2, cot_own, w1b, w2b, fwd, inv_nat)[0]


def per_device(latent, corr_kernel, w1, b1, w2, b2, cotangent):
    row_count, col_count, _ = latent.shape
    flip = flipped(lax.axis_index("zh"), lax.axis_index("c"))
    (send,) = call(send_kernel, [((PEERS, 32, CH), BF)], [((1024, CH), F4), ((1024, CH), F4)], 1 << 20, latent, cotangent)
    own = lax.all_to_all(send, ROWS_AXES, 0, 0, tiled=True)
    ring = device_ring()
    n = len(ring)
    everywhere = ROWS_AXES + COLS_AXES

    def shifted(block, by):
        return lax.ppermute(block, everywhere, [(ring[i], ring[(i + by) % n]) for i in range(n)])

    left, right = shifted(own, 1), shifted(own, -1)
    far_left, far_right = shifted(own[:, 8:16], 2), shifted(own[:, 0:8], -2)
    pred_send, *kept = forward(far_left, left, own, right, far_right, corr_kernel, w1, b1, w2, b2)
    pred_got = lax.all_to_all(pred_send, ROWS_AXES, 0, 0, tiled=True)
    grads = backward(w1, w2, *kept)
    grads, pred_got = lax.optimization_barrier((grads, pred_got))

    got = pred_got.reshape(4, 8, 4, row_count, CH)
    even, odd = got[:, 0::2], got[::-1, 1::2]
    got = jnp.stack([even, odd], axis=2).reshape(4, 8, 4, row_count, CH).transpose(1, 0, 2, 3, 4)
    got = got.reshape(PEERS, 4, row_count, CH)
    got = jnp.where(flip, got[::-1], got)
    pred_out = got.transpose(2, 0, 1, 3).reshape(row_count, col_count, CH)

    n_plane, n_depth = lax.axis_size(PLANE_AXES), lax.axis_size(DEPTH_AXES)
    share = GRAD_ROWS // n_plane
    part = lax.all_to_all(grads.reshape(n_plane, share, CH), PLANE_AXES, 0, 0, tiled=True)
    part = jnp.sum(part.astype(F4), axis=0).astype(BF)
    part = lax.all_to_all(jnp.broadcast_to(part, (n_depth, share, CH)), DEPTH_AXES, 0, 0, tiled=True)
    part = jnp.sum(part.astype(F4), axis=0).astype(BF)
    whole = lax.all_to_all(jnp.broadcast_to(part, (n_plane, share, CH)), PLANE_AXES, 0, 0, tiled=True)
    whole = whole.reshape(GRAD_ROWS, CH).astype(F4)
    dw1, dw2 = (whole[a : a + 1152].reshape(3, 3, CH, CH) for a in (0, 1152))
    return pred_out, dw1, whole[2432] + whole[2433], dw2, whole[2434] + whole[2435], whole[2304:2432]


def solution(mesh):
    split = Mesh(mesh.devices.reshape(tuple(SIZES[a] for a in ROWS_AXES + COLS_AXES)), ROWS_AXES + COLS_AXES)
    grid = P(ROWS_AXES, COLS_AXES, None)
    return jax.shard_map(
        per_device, mesh=split, in_specs=(grid, P(), P(), P(), P(), P(), grid),
        out_specs=(grid, P(), P(), P(), P(), P()), check_vma=False,
    )
```

```python
import jax
import jax.numpy as jnp
import numpy as np
from jax import lax
from jax.experimental import pallas as pl
from jax.experimental.pallas import tpu as pltpu
from jax.sharding import Mesh, PartitionSpec as P

ROWS_AXES = ("y", "zl")
COLS_AXES = ("x", "zh", "c")
PLANE_AXES = ("y", "x", "c")
DEPTH_AXES = ("zl", "zh")
SIZES = {"y": 4, "zl": 8, "x": 4, "zh": 2, "c": 2}
N_ROWS = 128
CH = 128
PEERS = 32
GRAD_ROWS = 2560
BF, F4 = jnp.bfloat16, jnp.float32
VMEM = pl.BlockSpec(memory_space=pltpu.VMEM)


def real_transform(order):
    freq = np.arange(64)
    angle = 2.0 * np.pi * ((freq[:, None] * order[None, :]) % N_ROWS) / N_ROWS
    sines = np.sin(angle)
    sines[0] = np.cos(np.pi * order)
    return np.concatenate([np.cos(angle), sines])


def split_two(table):
    high = table.astype(jnp.bfloat16)
    low = (table - high.astype(np.float64)).astype(jnp.bfloat16)
    return high, low


def tables():
    place = np.arange(N_ROWS)
    order = 4 * (place % 32) + place // 32
    weight = np.full((N_ROWS, 1), 2.0 / N_ROWS)
    weight[0] = weight[64] = 1.0 / N_ROWS
    made = []
    for rows in (order, place):
        made.append(np.concatenate(split_two(real_transform(rows)), axis=1))
        high, low = split_two((real_transform(rows) * weight).T)
        made.append(np.concatenate([high, high, low], axis=1))
    return made


def window_of(y, zl, flip):
    snake = zl * 4 + jnp.where(zl % 2 == 0, y, 3 - y)
    return jnp.where(flip, 31 - snake, snake)


def flipped(zh, c):
    return zh == c


def device_ring():
    ring = []
    for x in range(4):
        for zh in range(2):
            for c in range(2):
                block = [0] * 32
                for y in range(4):
                    for zl in range(8):
                        snake = zl * 4 + (y if zl % 2 == 0 else 3 - y)
                        block[31 - snake if flipped(zh, c) else snake] = (((y * 8 + zl) * 4 + x) * 2 + zh) * 2 + c
                ring += block
    return ring


def dot(a, b):
    return jnp.dot(a, b, preferred_element_type=F4)


def dot_t(a, b):
    return lax.dot_general(a, b, (((0,), (0,)), ((), ())), preferred_element_type=F4)


def turned(x, step):
    blocks = [x[32 * i : 32 * i + 32] for i in range(4)]
    if step > 0:
        moved = [pltpu.roll(b, 31, axis=0) for b in blocks[:step]]
        return jnp.concatenate(blocks[step:] + moved, axis=0)
    if step < 0:
        moved = [pltpu.roll(b, 1, axis=0) for b in blocks[step:]]
        return jnp.concatenate(moved + blocks[:step], axis=0)
    return x


def put_turned(ref, col, x, steps):
    for i, step in enumerate(steps):
        ref[col, :, i * CH : (i + 1) * CH] = turned(x, step).astype(BF)


def cross(first, second):
    fc, fs = first[:64], first[64:]
    sc, ss = second[:64], second[64:]
    real_row = lax.broadcasted_iota(jnp.int32, sc.shape, 0) == 0
    out_c = sc * fc + jnp.where(real_row, 0.0, ss * fs)
    out_s = jnp.where(real_row, ss * fs, ss * fc - sc * fs)
    return jnp.concatenate([out_c, out_s], axis=0)


def three_parts(x):
    high = x.astype(BF)
    low = (x - high.astype(F4)).astype(BF)
    return jnp.concatenate([high, low, high], axis=0)


def send_kernel(lat, cot, out, wide, packed):
    y, zl, zh, c = (lax.axis_index(a) for a in ("y", "zl", "zh", "c"))
    flip = flipped(zh, c)
    for t, ref in enumerate((lat, cot)):
        wide[t * 512 : t * 512 + 512, :] = ref[...].reshape(512, CH).astype(F4)
    for k in range(PEERS):
        start = pl.multiple_of(4 * window_of(k // 8, jnp.int32(k % 8), flip), 4)
        for t in range(2):
            for rr in range(4):
                piece = wide[pl.ds(t * 512 + rr * 128 + start, 4), :]
                packed[pl.ds(k * 32 + t * 16 + rr, 4, stride=4), :] = piece
    out[...] = packed[...].astype(BF).reshape(PEERS, 32, CH)


def column(ref, start, stride):
    return jnp.concatenate([ref[pl.ds(start + rr, 32, stride=stride), :] for rr in range(4)], axis=0)


def step_kernel(far_left, left, own, right, far_right, ker, w1, b1, w2, b2, w1b, w2b, fwd, inv, fwd_nat, inv_nat,
                pred, out,
                gl, go, gr, gl2, gr2, latf, xw, parts, cots, hid, placed, spec, m3, h3, rise1, slope2, s3, z3, gm):
    for ref, wide in ((left, gl), (own, go), (right, gr), (far_left, gl2), (far_right, gr2)):
        wide[...] = ref[...].reshape(wide.shape).astype(F4)
    lat_from = ([(gl2, 4, 8)] + [(gl, 4 * j, 32) for j in range(4)] + [(go, 4 * j, 32) for j in range(4)]
                + [(gr, 4 * j, 32) for j in range(4)] + [(gr2, 0, 8)])
    for j, (ref, start, stride) in enumerate(lat_from):
        x = column(ref, start, stride)
        latf[j] = x
        xb = x.astype(BF)
        xw[0:128, j * CH : (j + 1) * CH] = xb
        xw[128:256, j * CH : (j + 1) * CH] = xb
    cot_from = [(gl, 24), (gl, 28)] + [(go, 16 + 4 * j) for j in range(4)] + [(gr, 16), (gr, 20)]
    for u, (ref, start) in enumerate(cot_from):
        cots[u] = column(ref, start, 32)
    ker_two = jnp.concatenate([ker[...], ker[...]], axis=0)
    ker_spec = dot(fwd_nat[...], ker_two)
    for j in range(0, 14, 2):
        lanes = slice(j * CH, (j + 2) * CH)
        s = dot(fwd[...], xw[:, lanes])
        if 4 <= j < 10:
            spec[:, (j - 4) * CH : (j - 2) * CH] = s
        for i in range(2):
            part = s[:, i * CH : (i + 1) * CH]
            parts[:, i * CH : (i + 1) * CH] = three_parts(cross(ker_spec, part))
        corr = dot(inv[...], parts[...])
        for i in range(2):
            mixed = (latf[j + i] + corr[:, i * CH : (i + 1) * CH]).astype(BF).astype(F4)
            latf[j + i] = mixed
            put_turned(m3, j + i, mixed, (-1, 0, 1))
    for j in range(0, 12, 4):
        v = b1[...]
        for q in range(3):
            v = v + dot(m3[j + q : j + q + 4].reshape(512, 384), w1[q])
        g = jax.nn.sigmoid(v)
        if j == 4:
            rise1[...] = (g * (1.0 + v * (1.0 - g))).reshape(4, N_ROWS, CH)
        vg = v * g
        for i in range(4):
            h = (latf[j + i + 1] + vg[i * 128 : i * 128 + 128]).astype(BF).astype(F4)
            hid[j + i] = h
            put_turned(h3, j + i, h, (-2, 0, 2))
    for j in range(0, 8, 4):
        v = b2[...]
        for q in range(3):
            v = v + dot(h3[j + 2 * q : j + 2 * q + 4].reshape(512, 384), w2[q])
        g = jax.nn.sigmoid(v)
        vg = v * g
        rise = g * (1.0 + v * (1.0 - g))
        for i in range(4):
            u = j + i
            slope2[u] = (cots[u] * rise[i * 128 : i * 128 + 128]).astype(BF)
            if 2 <= u < 6:
                p = hid[u + 2] + vg[i * 128 : i * 128 + 128]
                for rr in range(4):
                    placed[pl.ds((u - 2) * 4 + rr, 32, stride=16), :] = p[rr * 32 : rr * 32 + 32]
    pred[...] = placed[...].astype(BF).reshape(PEERS, 16, CH)

    own2 = slope2[2:6].reshape(512, CH)
    for q in range(3):
        d = dot_t(h3[2 + 2 * q : 6 + 2 * q].reshape(512, 384), own2)
        for p in range(3):
            out[1152 + (p * 3 + q) * 128 : 1280 + (p * 3 + q) * 128, :] = d[p * 128 : p * 128 + 128].astype(BF)
    for u in range(8):
        put_turned(s3, u, slope2[u].astype(F4), (2, 0, -2))
    gh = cots[2:6].reshape(512, CH)
    for q in range(3):
        gh = gh + dot(s3[4 - 2 * q : 8 - 2 * q].reshape(512, 384), w2b[q])
    slope1 = (gh * rise1[...].reshape(512, CH)).astype(BF)
    slope1_wide = slope1.astype(F4)
    for i in range(4):
        put_turned(z3, i, slope1_wide[i * 128 : i * 128 + 128], (1, 0, -1))
    gm[0] = jnp.zeros((N_ROWS, CH), F4)
    gm[5] = jnp.zeros((N_ROWS, CH), F4)
    gm[1:5] = gh.reshape(4, N_ROWS, CH)
    for q in range(3):
        gm[q : q + 4] += dot(z3[...].reshape(512, 384), w1b[q]).reshape(4, N_ROWS, CH)
    for q in range(3):
        d = dot_t(m3[4 + q : 8 + q].reshape(512, 384), slope1)
        for p in range(3):
            out[(p * 3 + q) * 128 : (p * 3 + q) * 128 + 128, :] = d[p * 128 : p * 128 + 128].astype(BF)
    both = jnp.zeros((N_ROWS, CH), F4)
    for j in range(0, 6, 2):
        two = jnp.concatenate([gm[j], gm[j + 1]], axis=1).astype(BF)
        s = dot(fwd[...], jnp.concatenate([two, two], axis=0))
        for i in range(2):
            both = both + cross(s[:, i * CH : (i + 1) * CH], spec[:, (j + i) * CH : (j + i + 1) * CH])
    dk = dot(inv_nat[...], three_parts(both))
    out[2304:2432, :] = dk.astype(BF)
    db1 = jnp.sum(slope1_wide, axis=0, keepdims=True)
    db2 = jnp.sum(own2.astype(F4), axis=0, keepdims=True)
    rows = []
    for b in (db1, db2):
        high = b.astype(BF).astype(F4)
        rows += [high, b - high]
    tail = jnp.concatenate(rows + [jnp.zeros((GRAD_ROWS - 2436, CH), F4)], axis=0)
    out[2432:GRAD_ROWS, :] = tail.astype(BF)


def finish_kernel(whole, dw1, dw2, dk, db1, db2):
    rows = whole[...].reshape(GRAD_ROWS, CH)
    dw1[...] = rows[0:1152].astype(F4)
    dw2[...] = rows[1152:2304].astype(F4)
    dk[...] = rows[2304:2432].astype(F4)
    tail = rows[2432:2448].astype(F4)
    db1[...] = tail[0:1] + tail[1:2]
    db2[...] = tail[2:3] + tail[3:4]


def call(kernel, outs, scratch, flops, mib, *args):
    return pl.pallas_call(
        kernel,
        out_shape=[jax.ShapeDtypeStruct(s, d) for s, d in outs],
        in_specs=[VMEM] * len(args),
        out_specs=[VMEM] * len(outs),
        scratch_shapes=[pltpu.VMEM(s, d) for s, d in scratch],
        compiler_params=pltpu.CompilerParams(vmem_limit_bytes=mib << 20),
        cost_estimate=pl.CostEstimate(flops=flops, bytes_accessed=4 << 20, transcendentals=0),
    )(*args)


def local_step(far_left, left, own, right, far_right, ker, w1, b1, w2, b2):
    fwd, inv, fwd_nat, inv_nat = (jnp.asarray(t, BF) for t in tables())
    w1q, w2q = (w.transpose(1, 0, 2, 3).reshape(3, 384, CH) for w in (w1, w2))
    w1b, w2b = (w.transpose(1, 0, 3, 2).reshape(3, 384, CH) for w in (w1, w2))
    outs = [((PEERS, 16, CH), BF), ((GRAD_ROWS, CH), BF)]
    scratch = [((1024, CH), F4)] * 3 + [((256, CH), F4)] * 2 + [
        ((14, 128, CH), F4), ((256, 14 * CH), BF), ((384, 2 * CH), BF), ((8, 128, CH), F4), ((12, 128, CH), F4),
        ((512, CH), F4),
        ((128, 6 * CH), F4), ((14, 128, 384), BF), ((12, 128, 384), BF), ((4, 128, CH), F4), ((8, 128, CH), BF),
        ((8, 128, 384), BF), ((4, 128, 384), BF), ((6, 128, CH), F4)]
    return call(step_kernel, outs, scratch, 3 << 30, 24, far_left, left, own, right, far_right, ker,
                w1q, b1.reshape(1, CH), w2q, b2.reshape(1, CH), w1b, w2b, fwd, inv, fwd_nat, inv_nat)


def depth_sum(part):
    def moved(x, target):
        flat = [(z % 8) * 2 + z // 8 for z in range(16)]
        return lax.ppermute(x, DEPTH_AXES, [(flat[z], flat[target(z)]) for z in range(16)])

    opposite, ahead, behind = (moved(part, lambda z, d=d: (z + d) % 16) for d in (8, 4, 12))
    part = (part + opposite) + (ahead + behind)
    one, two, three = (moved(part, lambda z, d=d: z ^ d) for d in (1, 2, 3))
    return (part + one) + (two + three)


def per_device(latent, corr_kernel, w1, b1, w2, b2, cotangent):
    row_count, col_count, _ = latent.shape
    flip = flipped(lax.axis_index("zh"), lax.axis_index("c"))
    (send,) = call(send_kernel, [((PEERS, 32, CH), BF)], [((1024, CH), F4), ((1024, CH), F4)], 1 << 20, 4, latent, cotangent)
    own = lax.all_to_all(send, ROWS_AXES, 0, 0, tiled=True)
    ring = device_ring()
    n = len(ring)
    everywhere = ROWS_AXES + COLS_AXES

    def shifted(block, by):
        return lax.ppermute(block, everywhere, [(ring[i], ring[(i + by) % n]) for i in range(n)])

    left, right = shifted(own, 1), shifted(own, -1)
    far_left, far_right = shifted(own[:, 8:16], 2), shifted(own[:, 0:8], -2)
    pred_send, grads = local_step(far_left, left, own, right, far_right, corr_kernel, w1, b1, w2, b2)
    n_plane = lax.axis_size(PLANE_AXES)
    share = GRAD_ROWS // n_plane
    part = lax.all_to_all(grads.reshape(n_plane, share, CH), PLANE_AXES, 0, 0, tiled=True)
    part, pred_send = lax.optimization_barrier((part, pred_send))
    pred_got = lax.all_to_all(pred_send, ROWS_AXES, 0, 0, tiled=True)
    part = depth_sum(jnp.sum(part.astype(F4), axis=0)).astype(BF)
    part, pred_got = lax.optimization_barrier((part, pred_got))
    whole = lax.all_to_all(jnp.broadcast_to(part, (n_plane, share, CH)), PLANE_AXES, 0, 0, tiled=True)

    got = pred_got.reshape(4, 8, 4, row_count, CH)
    even, odd = got[:, 0::2], got[::-1, 1::2]
    got = jnp.stack([even, odd], axis=2).reshape(4, 8, 4, row_count, CH).transpose(1, 0, 2, 3, 4)
    got = got.reshape(PEERS, 4, row_count, CH)
    got = jnp.where(flip, got[::-1], got)
    pred_out = got.transpose(2, 0, 1, 3).reshape(row_count, col_count, CH)

    shapes = [(1152, CH), (1152, CH), (CH, CH), (1, CH), (1, CH)]
    dw1, dw2, dk, db1, db2 = call(finish_kernel, [(shape, F4) for shape in shapes], [], 1 << 20, 8, whole)
    grad_shape = (3, 3, CH, CH)
    return pred_out, dw1.reshape(grad_shape), db1.reshape(CH), dw2.reshape(grad_shape), db2.reshape(CH), dk


def solution(mesh):
    split = Mesh(mesh.devices.reshape(tuple(SIZES[a] for a in ROWS_AXES + COLS_AXES)), ROWS_AXES + COLS_AXES)
    grid = P(ROWS_AXES, COLS_AXES, None)
    return jax.shard_map(
        per_device, mesh=split, in_specs=(grid, P(), P(), P(), P(), P(), grid),
        out_specs=(grid, P(), P(), P(), P(), P()), check_vma=False,
    )
```

```python
import jax
import jax.numpy as jnp
import numpy as np
from jax import lax
from jax.experimental import pallas as pl
from jax.experimental.pallas import tpu as pltpu
from jax.sharding import Mesh, PartitionSpec as P

ROWS_AXES = ("y", "zl")
COLS_AXES = ("x", "zh", "c")
PLANE_AXES = ("y", "x", "c")
DEPTH_AXES = ("zl", "zh")
SIZES = {"y": 4, "zl": 8, "x": 4, "zh": 2, "c": 2}
N_ROWS = 128
CH = 128
PEERS = 32
GRAD_ROWS = 2560
BF, F4 = jnp.bfloat16, jnp.float32
VMEM = pl.BlockSpec(memory_space=pltpu.VMEM)


def real_transform(order):
    freq = np.arange(64)
    angle = 2.0 * np.pi * ((freq[:, None] * order[None, :]) % N_ROWS) / N_ROWS
    sines = np.sin(angle)
    sines[0] = np.cos(np.pi * order)
    return np.concatenate([np.cos(angle), sines])


def split_two(table):
    high = table.astype(jnp.bfloat16)
    low = (table - high.astype(np.float64)).astype(jnp.bfloat16)
    return high, low


def tables():
    place = np.arange(N_ROWS)
    order = 4 * (place % 32) + place // 32
    weight = np.full((N_ROWS, 1), 2.0 / N_ROWS)
    weight[0] = weight[64] = 1.0 / N_ROWS
    made = []
    for rows in (order, place):
        made.append(np.concatenate(split_two(real_transform(rows)), axis=1))
        high, low = split_two((real_transform(rows) * weight).T)
        made.append(np.concatenate([high, high, low], axis=1))
    return made


def window_of(y, zl, flip):
    snake = zl * 4 + jnp.where(zl % 2 == 0, y, 3 - y)
    return jnp.where(flip, 31 - snake, snake)


def flipped(zh, c):
    return zh == c


def device_ring():
    ring = []
    for x in range(4):
        for zh in range(2):
            for c in range(2):
                block = [0] * 32
                for y in range(4):
                    for zl in range(8):
                        snake = zl * 4 + (y if zl % 2 == 0 else 3 - y)
                        block[31 - snake if flipped(zh, c) else snake] = (((y * 8 + zl) * 4 + x) * 2 + zh) * 2 + c
                ring += block
    return ring


def dot(a, b):
    return jnp.dot(a, b, preferred_element_type=F4)


def dot_t(a, b):
    return lax.dot_general(a, b, (((0,), (0,)), ((), ())), preferred_element_type=F4)


def turned(x, step):
    blocks = [x[32 * i : 32 * i + 32] for i in range(4)]
    if step > 0:
        moved = [pltpu.roll(b, 31, axis=0) for b in blocks[:step]]
        return jnp.concatenate(blocks[step:] + moved, axis=0)
    if step < 0:
        moved = [pltpu.roll(b, 1, axis=0) for b in blocks[step:]]
        return jnp.concatenate(moved + blocks[:step], axis=0)
    return x


def put_turned(ref, col, x, steps):
    for i, step in enumerate(steps):
        ref[col, :, i * CH : (i + 1) * CH] = turned(x, step).astype(BF)


def cross(first, second):
    fc, fs = first[:64], first[64:]
    sc, ss = second[:64], second[64:]
    real_row = lax.broadcasted_iota(jnp.int32, sc.shape, 0) == 0
    out_c = sc * fc + jnp.where(real_row, 0.0, ss * fs)
    out_s = jnp.where(real_row, ss * fs, ss * fc - sc * fs)
    return jnp.concatenate([out_c, out_s], axis=0)


def three_parts(x):
    high = x.astype(BF)
    low = (x - high.astype(F4)).astype(BF)
    return jnp.concatenate([high, low, high], axis=0)


def send_kernel(lat, cot, out, wide, packed):
    y, zl, zh, c = (lax.axis_index(a) for a in ("y", "zl", "zh", "c"))
    flip = flipped(zh, c)
    for t, ref in enumerate((lat, cot)):
        wide[t * 512 : t * 512 + 512, :] = ref[...].reshape(512, CH).astype(F4)
    for k in range(PEERS):
        start = pl.multiple_of(4 * window_of(k // 8, jnp.int32(k % 8), flip), 4)
        for t in range(2):
            for rr in range(4):
                piece = wide[pl.ds(t * 512 + rr * 128 + start, 4), :]
                packed[pl.ds(k * 32 + t * 16 + rr, 4, stride=4), :] = piece
    out[...] = packed[...].astype(BF).reshape(PEERS, 32, CH)


def column(ref, start, stride):
    return jnp.concatenate([ref[pl.ds(start + rr, 32, stride=stride), :] for rr in range(4)], axis=0)


def step_kernel(left, own, right, ker, w1, b1, w2, b2, w1b, w2b, fwd, inv, fwd_nat, inv_nat,
                pred, out,
                gl, go, gr, latf, xw, parts, cots, hid, placed, spec, m3, h3, rise1, s3, z3, gh, gm):
    for ref, wide in ((left, gl), (own, go), (right, gr)):
        wide[...] = ref[...].reshape(wide.shape).astype(F4)
    lat_from = ([(gl, 4 * j, 16) for j in (1, 2, 3)] + [(go, 4 * j, 32) for j in range(4)]
                + [(gr, 4 * j, 16) for j in (0, 1, 2)])
    for j, (ref, start, stride) in enumerate(lat_from):
        x = column(ref, start, stride)
        latf[j] = x
        xb = x.astype(BF)
        xw[0:128, j * CH : (j + 1) * CH] = xb
        xw[128:256, j * CH : (j + 1) * CH] = xb
    for u in range(4):
        cots[u] = column(go, 16 + 4 * u, 32)
    ker_spec = dot(fwd_nat[...], jnp.concatenate([ker[...], ker[...]], axis=0))
    for j in range(0, 10, 2):
        lanes = slice(j * CH, (j + 2) * CH)
        s = dot(fwd[...], xw[:, lanes])
        spec[:, lanes] = s
        for i in range(2):
            parts[:, i * CH : (i + 1) * CH] = three_parts(cross(ker_spec, s[:, i * CH : (i + 1) * CH]))
        corr = dot(inv[...], parts[...])
        for i in range(2):
            mixed = (latf[j + i] + corr[:, i * CH : (i + 1) * CH]).astype(BF).astype(F4)
            latf[j + i] = mixed
            put_turned(m3, j + i, mixed, (-1, 0, 1))
    for j in range(0, 8, 4):
        v = b1[...]
        for q in range(3):
            v = v + dot(m3[j + q : j + q + 4].reshape(512, 384), w1[q])
        g = jax.nn.sigmoid(v)
        rise1[j * 128 : j * 128 + 512, :] = g * (1.0 + v * (1.0 - g))
        vg = v * g
        for i in range(4):
            h = (latf[j + i + 1] + vg[i * 128 : i * 128 + 128]).astype(BF).astype(F4)
            hid[j + i] = h
            put_turned(h3, j + i, h, (-2, 0, 2))
    v = b2[...]
    for q in range(3):
        v = v + dot(h3[2 * q : 2 * q + 4].reshape(512, 384), w2[q])
    g = jax.nn.sigmoid(v)
    p = hid[2:6].reshape(512, CH) + v * g
    for u in range(4):
        for rr in range(4):
            placed[pl.ds(u * 4 + rr, 32, stride=16), :] = p[u * 128 + rr * 32 : u * 128 + rr * 32 + 32]
    pred[...] = placed[...].astype(BF).reshape(PEERS, 16, CH)
    cot = cots[...].reshape(512, CH)
    own2 = (cot * (g * (1.0 + v * (1.0 - g)))).astype(BF)
    own2_wide = own2.astype(F4)
    for u in range(4):
        put_turned(s3, u, own2_wide[u * 128 : u * 128 + 128], (2, 0, -2))
    gh[...] = jnp.zeros(gh.shape, F4)
    gh[256:768, :] = cot
    for q in range(3):
        gh[q * 256 : q * 256 + 512, :] += dot(s3[...].reshape(512, 384), w2b[q])
    slope1 = (gh[...] * rise1[...]).astype(BF)
    slope1_wide = slope1.astype(F4)
    for u in range(8):
        put_turned(z3, u, slope1_wide[u * 128 : u * 128 + 128], (1, 0, -1))
    gm[...] = jnp.zeros(gm.shape, F4)
    gm[128:1152, :] = gh[...]
    for q in range(3):
        gm[q * 128 : q * 128 + 1024, :] += dot(z3[...].reshape(1024, 384), w1b[q])
    for q in range(3):
        d = dot_t(m3[q : q + 8].reshape(1024, 384), slope1)
        e = dot_t(h3[2 * q : 2 * q + 4].reshape(512, 384), own2)
        for p in range(3):
            at = (p * 3 + q) * 128
            out[at : at + 128, :] = d[p * 128 : p * 128 + 128].astype(BF)
            out[1152 + at : 1280 + at, :] = e[p * 128 : p * 128 + 128].astype(BF)
    both = jnp.zeros((N_ROWS, CH), F4)
    for j in range(0, 10, 2):
        two = jnp.concatenate([gm[(j + i) * 128 : (j + i) * 128 + 128, :] for i in range(2)], axis=1).astype(BF)
        s = dot(fwd[...], jnp.concatenate([two, two], axis=0))
        for i in range(2):
            both = both + cross(s[:, i * CH : (i + 1) * CH], spec[:, (j + i) * CH : (j + i + 1) * CH])
    out[2304:2432, :] = dot(inv_nat[...], three_parts(both)).astype(BF)
    rows = []
    for wide in (slope1_wide, own2_wide):
        b = jnp.sum(wide, axis=0, keepdims=True)
        high = b.astype(BF).astype(F4)
        rows += [high, b - high]
    tail = jnp.concatenate(rows + [jnp.zeros((GRAD_ROWS - 2436, CH), F4)], axis=0)
    out[2432:GRAD_ROWS, :] = tail.astype(BF)


def finish_kernel(whole, dw1, dw2, dk, db1, db2):
    rows = whole[...].reshape(GRAD_ROWS, CH)
    dw1[...] = rows[0:1152].astype(F4)
    dw2[...] = rows[1152:2304].astype(F4)
    dk[...] = rows[2304:2432].astype(F4)
    tail = rows[2432:2448].astype(F4)
    db1[...] = tail[0:1] + tail[1:2]
    db2[...] = tail[2:3] + tail[3:4]


def call(kernel, outs, scratch, flops, mib, *args):
    return pl.pallas_call(
        kernel,
        out_shape=[jax.ShapeDtypeStruct(s, d) for s, d in outs],
        in_specs=[VMEM] * len(args),
        out_specs=[VMEM] * len(outs),
        scratch_shapes=[pltpu.VMEM(s, d) for s, d in scratch],
        compiler_params=pltpu.CompilerParams(vmem_limit_bytes=mib << 20),
        cost_estimate=pl.CostEstimate(flops=flops, bytes_accessed=4 << 20, transcendentals=0),
    )(*args)


def local_step(left, own, right, ker, w1, b1, w2, b2):
    fwd, inv, fwd_nat, inv_nat = (jnp.asarray(t, BF) for t in tables())
    w1q, w2q = (w.transpose(1, 0, 2, 3).reshape(3, 384, CH) for w in (w1, w2))
    w1b, w2b = (w.transpose(1, 0, 3, 2).reshape(3, 384, CH) for w in (w1, w2))
    outs = [((PEERS, 16, CH), BF), ((GRAD_ROWS, CH), BF)]
    scratch = [((512, CH), F4), ((1024, CH), F4), ((512, CH), F4),
               ((10, 128, CH), F4), ((256, 10 * CH), BF), ((384, 2 * CH), BF), ((4, 128, CH), F4), ((8, 128, CH), F4),
               ((512, CH), F4), ((128, 10 * CH), F4), ((10, 128, 384), BF), ((8, 128, 384), BF), ((1024, CH), F4),
               ((4, 128, 384), BF), ((8, 128, 384), BF), ((1024, CH), F4), ((1280, CH), F4)]
    return call(step_kernel, outs, scratch, 3 << 30, 24, left, own, right, ker,
                w1q, b1.reshape(1, CH), w2q, b2.reshape(1, CH), w1b, w2b, fwd, inv, fwd_nat, inv_nat)


def depth_sum(part):
    def moved(x, target):
        flat = [(z % 8) * 2 + z // 8 for z in range(16)]
        return lax.ppermute(x, DEPTH_AXES, [(flat[z], flat[target(z)]) for z in range(16)])

    opposite, ahead, behind = (moved(part, lambda z, d=d: (z + d) % 16) for d in (8, 4, 12))
    part = (part + opposite) + (ahead + behind)
    one, two, three = (moved(part, lambda z, d=d: z ^ d) for d in (1, 2, 3))
    return (part + one) + (two + three)


def per_device(latent, corr_kernel, w1, b1, w2, b2, cotangent):
    row_count, col_count, _ = latent.shape
    flip = flipped(lax.axis_index("zh"), lax.axis_index("c"))
    block = pl.BlockSpec(latent.shape, lambda i: (0, 0, 0))
    send = pl.pallas_call(
        send_kernel,
        grid=(1,),
        out_shape=jax.ShapeDtypeStruct((PEERS, 32, CH), BF),
        in_specs=[block, block],
        out_specs=pl.BlockSpec((PEERS, 32, CH), lambda i: (0, 0, 0)),
        scratch_shapes=[pltpu.VMEM((1024, CH), F4), pltpu.VMEM((1024, CH), F4)],
        compiler_params=pltpu.CompilerParams(vmem_limit_bytes=60 << 20),
    )(latent, cotangent)
    own = lax.all_to_all(send, ROWS_AXES, 0, 0, tiled=True)
    ring = device_ring()
    n = len(ring)
    everywhere = ROWS_AXES + COLS_AXES

    def shifted(block, by):
        return lax.ppermute(block, everywhere, [(ring[i], ring[(i + by) % n]) for i in range(n)])

    left, right = shifted(own[:, 0:16], 1), shifted(own[:, 0:16], -1)
    pred_send, grads = local_step(left, own, right, corr_kernel, w1, b1, w2, b2)
    n_plane = lax.axis_size(PLANE_AXES)
    share = GRAD_ROWS // n_plane
    part = lax.all_to_all(grads.reshape(n_plane, share, CH), PLANE_AXES, 0, 0, tiled=True)
    part, pred_send = lax.optimization_barrier((part, pred_send))
    pred_got = lax.all_to_all(pred_send, ROWS_AXES, 0, 0, tiled=True)
    part = depth_sum(jnp.sum(part.astype(F4), axis=0)).astype(BF)
    part, pred_got = lax.optimization_barrier((part, pred_got))
    whole = lax.all_to_all(jnp.broadcast_to(part, (n_plane, share, CH)), PLANE_AXES, 0, 0, tiled=True)

    got = pred_got.reshape(4, 8, 4, row_count, CH)
    even, odd = got[:, 0::2], got[::-1, 1::2]
    got = jnp.stack([even, odd], axis=2).reshape(4, 8, 4, row_count, CH).transpose(1, 0, 2, 3, 4)
    got = got.reshape(PEERS, 4, row_count, CH)
    got = jnp.where(flip, got[::-1], got)
    pred_out = got.transpose(2, 0, 1, 3).reshape(row_count, col_count, CH)

    shapes = [(1152, CH), (1152, CH), (CH, CH), (1, CH), (1, CH)]
    dw1, dw2, dk, db1, db2 = call(finish_kernel, [(shape, F4) for shape in shapes], [], 1 << 20, 8, whole)
    grad_shape = (3, 3, CH, CH)
    return pred_out, dw1.reshape(grad_shape), db1.reshape(CH), dw2.reshape(grad_shape), db2.reshape(CH), dk


def solution(mesh):
    split = Mesh(mesh.devices.reshape(tuple(SIZES[a] for a in ROWS_AXES + COLS_AXES)), ROWS_AXES + COLS_AXES)
    grid = P(ROWS_AXES, COLS_AXES, None)
    return jax.shard_map(
        per_device, mesh=split, in_specs=(grid, P(), P(), P(), P(), P(), grid),
        out_specs=(grid, P(), P(), P(), P(), P()), check_vma=False,
    )
```

```python
import jax
import jax.numpy as jnp
import numpy as np
from jax import lax
from jax.experimental import pallas as pl
from jax.experimental.pallas import tpu as pltpu
from jax.sharding import Mesh, PartitionSpec as P

ROWS_AXES = ("y", "zb", "za")
COLS_AXES = ("x", "zh", "c")
PLANE_AXES = ("y", "za", "x", "c")
DEPTH_AXES = ("zb", "zh")
SIZES = {"y": 4, "zb": 4, "za": 2, "x": 4, "zh": 2, "c": 2}
N_ROWS = 128
CH = 128
PEERS = 32
GRAD_ROWS = 2560
BF, F4 = jnp.bfloat16, jnp.float32
VMEM = pl.BlockSpec(memory_space=pltpu.VMEM)


def real_transform(order):
    freq = np.arange(64)
    angle = 2.0 * np.pi * ((freq[:, None] * order[None, :]) % N_ROWS) / N_ROWS
    sines = np.sin(angle)
    sines[0] = np.cos(np.pi * order)
    return np.concatenate([np.cos(angle), sines])


def split_two(table):
    high = table.astype(jnp.bfloat16)
    low = (table - high.astype(np.float64)).astype(jnp.bfloat16)
    return high, low


def tables():
    place = np.arange(N_ROWS)
    order = 4 * (place % 32) + place // 32
    weight = np.full((N_ROWS, 1), 2.0 / N_ROWS)
    weight[0] = weight[64] = 1.0 / N_ROWS
    made = []
    for rows in (order, place):
        made.append(np.concatenate(split_two(real_transform(rows)), axis=1))
        high, low = split_two((real_transform(rows) * weight).T)
        made.append(np.concatenate([high, high, low], axis=1))
    return made


def window_of(y, zl, flip):
    snake = zl * 4 + jnp.where(zl % 2 == 0, y, 3 - y)
    return jnp.where(flip, 31 - snake, snake)


def flipped(zh, c):
    return zh == c


def device_ring():
    ring = []
    for x in range(4):
        for zh in range(2):
            for c in range(2):
                block = [0] * 32
                for y in range(4):
                    for zl in range(8):
                        snake = zl * 4 + (y if zl % 2 == 0 else 3 - y)
                        block[31 - snake if flipped(zh, c) else snake] = (((y * 8 + zl) * 4 + x) * 2 + zh) * 2 + c
                ring += block
    return ring


def dot(a, b):
    return jnp.dot(a, b, preferred_element_type=F4)


def dot_t(a, b):
    return lax.dot_general(a, b, (((0,), (0,)), ((), ())), preferred_element_type=F4)


def turned(x, step):
    blocks = [x[32 * i : 32 * i + 32] for i in range(4)]
    if step > 0:
        moved = [pltpu.roll(b, 31, axis=0) for b in blocks[:step]]
        return jnp.concatenate(blocks[step:] + moved, axis=0)
    if step < 0:
        moved = [pltpu.roll(b, 1, axis=0) for b in blocks[step:]]
        return jnp.concatenate(moved + blocks[:step], axis=0)
    return x


def put_turned(ref, col, x, steps):
    for i, step in enumerate(steps):
        ref[col, :, i * CH : (i + 1) * CH] = turned(x, step).astype(BF)


def cross(first, second):
    fc, fs = first[:64], first[64:]
    sc, ss = second[:64], second[64:]
    real_row = lax.broadcasted_iota(jnp.int32, sc.shape, 0) == 0
    out_c = sc * fc + jnp.where(real_row, 0.0, ss * fs)
    out_s = jnp.where(real_row, ss * fs, ss * fc - sc * fs)
    return jnp.concatenate([out_c, out_s], axis=0)


def three_parts(x):
    high = x.astype(BF)
    low = (x - high.astype(F4)).astype(BF)
    return jnp.concatenate([high, low, high], axis=0)


def send_kernel(lat, cot, out, wide, packed):
    zh, c = lax.axis_index("zh"), lax.axis_index("c")
    flip = flipped(zh, c)
    for t, ref in enumerate((lat, cot)):
        wide[t * 512 : t * 512 + 512, :] = ref[...].reshape(512, CH).astype(F4)
    for k in range(PEERS):
        start = pl.multiple_of(4 * window_of(k // 8, jnp.int32(k % 8), flip), 4)
        for t in range(2):
            for rr in range(4):
                piece = wide[pl.ds(t * 512 + rr * 128 + start, 4), :]
                packed[pl.ds(k * 32 + t * 16 + rr, 4, stride=4), :] = piece
    out[...] = packed[...].astype(BF).reshape(PEERS, 32, CH)


def column(ref, start, stride):
    return jnp.concatenate([ref[pl.ds(start + rr, 32, stride=stride), :] for rr in range(4)], axis=0)


def step_kernel(left, own, right, ker, w1, b1, w2, b2, w1b, w2b, fwd, inv, fwd_nat, inv_nat,
                pred, out,
                gl, go, gr, latf, xw, parts, cots, hid, placed, spec, m3, h3, rise1, s3, z3, gh, gm):
    for ref, wide in ((left, gl), (own, go), (right, gr)):
        wide[...] = ref[...].reshape(wide.shape).astype(F4)
    lat_from = ([(gl, 4 * j, 16) for j in (1, 2, 3)] + [(go, 4 * j, 32) for j in range(4)]
                + [(gr, 4 * j, 16) for j in (0, 1, 2)])
    for j, (ref, start, stride) in enumerate(lat_from):
        x = column(ref, start, stride)
        latf[j] = x
        xb = x.astype(BF)
        xw[0:128, j * CH : (j + 1) * CH] = xb
        xw[128:256, j * CH : (j + 1) * CH] = xb
    for u in range(4):
        cots[u] = column(go, 16 + 4 * u, 32)
    ker_spec = dot(fwd_nat[...], jnp.concatenate([ker[...], ker[...]], axis=0))
    for j in range(0, 10, 2):
        lanes = slice(j * CH, (j + 2) * CH)
        s = dot(fwd[...], xw[:, lanes])
        spec[:, lanes] = s
        for i in range(2):
            parts[:, i * CH : (i + 1) * CH] = three_parts(cross(ker_spec, s[:, i * CH : (i + 1) * CH]))
        corr = dot(inv[...], parts[...])
        for i in range(2):
            mixed = (latf[j + i] + corr[:, i * CH : (i + 1) * CH]).astype(BF).astype(F4)
            latf[j + i] = mixed
            put_turned(m3, j + i, mixed, (-1, 0, 1))
    for j in range(0, 8, 4):
        v = b1[...]
        for q in range(3):
            v = v + dot(m3[j + q : j + q + 4].reshape(512, 384), w1[q])
        g = jax.nn.sigmoid(v)
        rise1[j * 128 : j * 128 + 512, :] = g * (1.0 + v * (1.0 - g))
        vg = v * g
        for i in range(4):
            h = (latf[j + i + 1] + vg[i * 128 : i * 128 + 128]).astype(BF).astype(F4)
            hid[j + i] = h
            put_turned(h3, j + i, h, (-2, 0, 2))
    v = b2[...]
    for q in range(3):
        v = v + dot(h3[2 * q : 2 * q + 4].reshape(512, 384), w2[q])
    g = jax.nn.sigmoid(v)
    p = hid[2:6].reshape(512, CH) + v * g
    for u in range(4):
        for rr in range(4):
            placed[pl.ds(u * 4 + rr, 32, stride=16), :] = p[u * 128 + rr * 32 : u * 128 + rr * 32 + 32]
    pred[...] = placed[...].astype(BF).reshape(PEERS, 16, CH)
    cot = cots[...].reshape(512, CH)
    own2 = (cot * (g * (1.0 + v * (1.0 - g)))).astype(BF)
    own2_wide = own2.astype(F4)
    for u in range(4):
        put_turned(s3, u, own2_wide[u * 128 : u * 128 + 128], (2, 0, -2))
    gh[...] = jnp.zeros(gh.shape, F4)
    gh[256:768, :] = cot
    for q in range(3):
        gh[q * 256 : q * 256 + 512, :] += dot(s3[...].reshape(512, 384), w2b[q])
    slope1 = (gh[...] * rise1[...]).astype(BF)
    slope1_wide = slope1.astype(F4)
    for u in range(8):
        put_turned(z3, u, slope1_wide[u * 128 : u * 128 + 128], (1, 0, -1))
    gm[...] = jnp.zeros(gm.shape, F4)
    gm[128:1152, :] = gh[...]
    for q in range(3):
        gm[q * 128 : q * 128 + 1024, :] += dot(z3[...].reshape(1024, 384), w1b[q])
    for q in range(3):
        d = dot_t(m3[q : q + 8].reshape(1024, 384), slope1)
        e = dot_t(h3[2 * q : 2 * q + 4].reshape(512, 384), own2)
        for p in range(3):
            at = (p * 3 + q) * 128
            out[at : at + 128, :] = d[p * 128 : p * 128 + 128].astype(BF)
            out[1152 + at : 1280 + at, :] = e[p * 128 : p * 128 + 128].astype(BF)
    both = jnp.zeros((N_ROWS, CH), F4)
    for j in range(0, 10, 2):
        two = jnp.concatenate([gm[(j + i) * 128 : (j + i) * 128 + 128, :] for i in range(2)], axis=1).astype(BF)
        s = dot(fwd[...], jnp.concatenate([two, two], axis=0))
        for i in range(2):
            both = both + cross(s[:, i * CH : (i + 1) * CH], spec[:, (j + i) * CH : (j + i + 1) * CH])
    out[2304:2432, :] = dot(inv_nat[...], three_parts(both)).astype(BF)
    rows = []
    for wide in (slope1_wide, own2_wide):
        b = jnp.sum(wide, axis=0, keepdims=True)
        high = b.astype(BF).astype(F4)
        rows += [high, b - high]
    tail = jnp.concatenate(rows + [jnp.zeros((GRAD_ROWS - 2436, CH), F4)], axis=0)
    out[2432:GRAD_ROWS, :] = tail.astype(BF)


def finish_kernel(whole, dw1, dw2, dk, db1, db2):
    dw1[...] = whole[0:1152].astype(F4)
    dw2[...] = whole[1152:2304].astype(F4)
    dk[...] = whole[2304:2432].astype(F4)
    tail = whole[2432:2448].astype(F4)
    db1[...] = tail[0:1] + tail[1:2]
    db2[...] = tail[2:3] + tail[3:4]


def call(kernel, outs, scratch, flops, mib, *args):
    return pl.pallas_call(
        kernel,
        out_shape=[jax.ShapeDtypeStruct(s, d) for s, d in outs],
        in_specs=[VMEM] * len(args),
        out_specs=[VMEM] * len(outs),
        scratch_shapes=[pltpu.VMEM(s, d) for s, d in scratch],
        compiler_params=pltpu.CompilerParams(vmem_limit_bytes=mib << 20),
        cost_estimate=pl.CostEstimate(flops=flops, bytes_accessed=4 << 20, transcendentals=0),
    )(*args)


def local_step(left, own, right, ker, w1, b1, w2, b2):
    fwd, inv, fwd_nat, inv_nat = (jnp.asarray(t, BF) for t in tables())
    w1q, w2q = (w.transpose(1, 0, 2, 3).reshape(3, 384, CH) for w in (w1, w2))
    w1b, w2b = (w.transpose(1, 0, 3, 2).reshape(3, 384, CH) for w in (w1, w2))
    outs = [((PEERS, 16, CH), BF), ((GRAD_ROWS, CH), BF)]
    scratch = [((512, CH), F4), ((1024, CH), F4), ((512, CH), F4),
               ((10, 128, CH), F4), ((256, 10 * CH), BF), ((384, 2 * CH), BF), ((4, 128, CH), F4), ((8, 128, CH), F4),
               ((512, CH), F4), ((128, 10 * CH), F4), ((10, 128, 384), BF), ((8, 128, 384), BF), ((1024, CH), F4),
               ((4, 128, 384), BF), ((8, 128, 384), BF), ((1024, CH), F4), ((1280, CH), F4)]
    return call(step_kernel, outs, scratch, 3 << 30, 24, left, own, right, ker,
                w1q, b1.reshape(1, CH), w2q, b2.reshape(1, CH), w1b, w2b, fwd, inv, fwd_nat, inv_nat)


def sum_kernel(got, out):
    total = got[0].astype(F4)
    for i in range(1, got.shape[0]):
        total = total + got[i].astype(F4)
    total = total.astype(BF)
    for i in range(out.shape[0]):
        out[i] = total


def summed(got, copies):
    (out,) = call(sum_kernel, [((copies,) + got.shape[1:], BF)], [], 1 << 20, 8, got)
    return out


def per_device(latent, corr_kernel, w1, b1, w2, b2, cotangent):
    row_count, col_count, _ = latent.shape
    flip = flipped(lax.axis_index("zh"), lax.axis_index("c"))
    block = pl.BlockSpec(latent.shape, lambda i: (0, 0, 0))
    send = pl.pallas_call(
        send_kernel,
        grid=(1,),
        out_shape=jax.ShapeDtypeStruct((PEERS, 32, CH), BF),
        in_specs=[block, block],
        out_specs=pl.BlockSpec((PEERS, 32, CH), lambda i: (0, 0, 0)),
        scratch_shapes=[pltpu.VMEM((1024, CH), F4), pltpu.VMEM((1024, CH), F4)],
        compiler_params=pltpu.CompilerParams(vmem_limit_bytes=60 << 20),
    )(latent, cotangent)
    own = lax.all_to_all(send, ROWS_AXES, 0, 0, tiled=True)
    ring = device_ring()
    n = len(ring)
    everywhere = ROWS_AXES + COLS_AXES

    def shifted(block, by):
        return lax.ppermute(block, everywhere, [(ring[i], ring[(i + by) % n]) for i in range(n)])

    left, right = shifted(own[:, 0:16], 1), shifted(own[:, 0:16], -1)
    pred_send, grads = local_step(left, own, right, corr_kernel, w1, b1, w2, b2)
    n_plane, n_depth = lax.axis_size(PLANE_AXES), lax.axis_size(DEPTH_AXES)
    part = lax.all_to_all(grads.reshape(n_plane, GRAD_ROWS // n_plane, CH), PLANE_AXES, 0, 0, tiled=True)
    part = lax.all_to_all(summed(part, n_depth), DEPTH_AXES, 0, 0, tiled=True)
    part, pred_send = lax.optimization_barrier((part, pred_send))
    pred_got = lax.all_to_all(pred_send, ROWS_AXES, 0, 0, tiled=True)
    part, pred_got = lax.optimization_barrier((summed(part, n_plane), pred_got))
    whole = lax.all_to_all(part, PLANE_AXES, 0, 0, tiled=True).reshape(GRAD_ROWS, CH)

    got = pred_got.reshape(4, 8, 4, row_count, CH)
    even, odd = got[:, 0::2], got[::-1, 1::2]
    got = jnp.stack([even, odd], axis=2).reshape(4, 8, 4, row_count, CH).transpose(1, 0, 2, 3, 4)
    got = got.reshape(PEERS, 4, row_count, CH)
    got = jnp.where(flip, got[::-1], got)
    pred_out = got.transpose(2, 0, 1, 3).reshape(row_count, col_count, CH)

    shapes = [(1152, CH), (1152, CH), (CH, CH), (1, CH), (1, CH)]
    dw1, dw2, dk, db1, db2 = call(finish_kernel, [(shape, F4) for shape in shapes], [], 1 << 20, 8, whole)
    grad_shape = (3, 3, CH, CH)
    return pred_out, dw1.reshape(grad_shape), db1.reshape(CH), dw2.reshape(grad_shape), db2.reshape(CH), dk


def solution(mesh):
    split = Mesh(mesh.devices.reshape(tuple(SIZES[a] for a in ROWS_AXES + COLS_AXES)), ROWS_AXES + COLS_AXES)
    grid = P(ROWS_AXES, COLS_AXES, None)
    return jax.shard_map(
        per_device, mesh=split, in_specs=(grid, P(), P(), P(), P(), P(), grid),
        out_specs=(grid, P(), P(), P(), P(), P()), check_vma=False,
    )
```

```python
import jax
import jax.numpy as jnp
import numpy as np
from jax import lax
from jax.experimental import pallas as pl
from jax.experimental.pallas import tpu as pltpu
from jax.sharding import Mesh, PartitionSpec as P

ROWS_AXES = ("y", "zb", "za")
COLS_AXES = ("x", "zh", "c")
NEAR_AXES = ("y", "za")
PLANE_AXES = ("c", "x", "y", "za")
DEPTH_AXES = ("zb", "zh")
SIZES = {"y": 4, "zb": 4, "za": 2, "x": 4, "zh": 2, "c": 2}
N_ROWS = 128
CH = 128
PEERS = 32
GRAD_ROWS = 2560
BF, F4 = jnp.bfloat16, jnp.float32
VMEM = pl.BlockSpec(memory_space=pltpu.VMEM)


def real_transform(order):
    freq = np.arange(64)
    angle = 2.0 * np.pi * ((freq[:, None] * order[None, :]) % N_ROWS) / N_ROWS
    sines = np.sin(angle)
    sines[0] = np.cos(np.pi * order)
    return np.concatenate([np.cos(angle), sines])


def split_two(table):
    high = table.astype(jnp.bfloat16)
    low = (table - high.astype(np.float64)).astype(jnp.bfloat16)
    return high, low


def tables():
    place = np.arange(N_ROWS)
    order = 4 * (place % 32) + place // 32
    weight = np.full((N_ROWS, 1), 2.0 / N_ROWS)
    weight[0] = weight[64] = 1.0 / N_ROWS
    made = []
    for rows in (order, place):
        made.append(np.concatenate(split_two(real_transform(rows)), axis=1))
        high, low = split_two((real_transform(rows) * weight).T)
        made.append(np.concatenate([high, high, low], axis=1))
    return made


def window_of(y, zl, flip):
    snake = zl * 4 + jnp.where(zl % 2 == 0, y, 3 - y)
    return jnp.where(flip, 31 - snake, snake)


def flipped(zh, c):
    return zh == c


def device_ring():
    ring = []
    for x in range(4):
        for zh in range(2):
            for c in range(2):
                block = [0] * 32
                for y in range(4):
                    for zl in range(8):
                        snake = zl * 4 + (y if zl % 2 == 0 else 3 - y)
                        block[31 - snake if flipped(zh, c) else snake] = (((y * 8 + zl) * 4 + x) * 2 + zh) * 2 + c
                ring += block
    return ring


def dot(a, b):
    return jnp.dot(a, b, preferred_element_type=F4)


def dot_t(a, b):
    return lax.dot_general(a, b, (((0,), (0,)), ((), ())), preferred_element_type=F4)


def turned(x, step):
    blocks = [x[32 * i : 32 * i + 32] for i in range(4)]
    if step > 0:
        moved = [pltpu.roll(b, 31, axis=0) for b in blocks[:step]]
        return jnp.concatenate(blocks[step:] + moved, axis=0)
    if step < 0:
        moved = [pltpu.roll(b, 1, axis=0) for b in blocks[step:]]
        return jnp.concatenate(moved + blocks[:step], axis=0)
    return x


def put_turned(ref, col, x, steps):
    for i, step in enumerate(steps):
        ref[col, :, i * CH : (i + 1) * CH] = turned(x, step).astype(BF)


def cross(first, second):
    fc, fs = first[:64], first[64:]
    sc, ss = second[:64], second[64:]
    real_row = lax.broadcasted_iota(jnp.int32, sc.shape, 0) == 0
    out_c = sc * fc + jnp.where(real_row, 0.0, ss * fs)
    out_s = jnp.where(real_row, ss * fs, ss * fc - sc * fs)
    return jnp.concatenate([out_c, out_s], axis=0)


def three_parts(x):
    high = x.astype(BF)
    low = (x - high.astype(F4)).astype(BF)
    return jnp.concatenate([high, low, high], axis=0)


def send_kernel(lat, cot, out, wide, packed):
    zh, c = lax.axis_index("zh"), lax.axis_index("c")
    flip = flipped(zh, c)
    for t, ref in enumerate((lat, cot)):
        wide[t * 512 : t * 512 + 512, :] = ref[...].reshape(512, CH).astype(F4)
    for k in range(PEERS):
        start = pl.multiple_of(4 * window_of(k // 8, jnp.int32(k % 8), flip), 4)
        for t in range(2):
            for rr in range(4):
                piece = wide[pl.ds(t * 512 + rr * 128 + start, 4), :]
                packed[pl.ds(k * 32 + t * 16 + rr, 4, stride=4), :] = piece
    out[...] = packed[...].astype(BF).reshape(PEERS, 32, CH)


def column(ref, start, stride):
    return jnp.concatenate([ref[pl.ds(start + rr, 32, stride=stride), :] for rr in range(4)], axis=0)


def step_kernel(left, own, right, ker, w1, b1, w2, b2, w1b, w2b, fwd, inv, fwd_nat, inv_nat,
                pred, keep, give,
                gl, go, gr, latf, xw, parts, cots, hid, placed, spec, m3, h3, rise1, s3, z3, gh, gm, halves):
    for ref, wide in ((left, gl), (own, go), (right, gr)):
        wide[...] = ref[...].reshape(wide.shape).astype(F4)
    lat_from = ([(gl, 4 * j, 16) for j in (1, 2, 3)] + [(go, 4 * j, 32) for j in range(4)]
                + [(gr, 4 * j, 16) for j in (0, 1, 2)])
    for j, (ref, start, stride) in enumerate(lat_from):
        x = column(ref, start, stride)
        latf[j] = x
        xb = x.astype(BF)
        xw[0:128, j * CH : (j + 1) * CH] = xb
        xw[128:256, j * CH : (j + 1) * CH] = xb
    for u in range(4):
        cots[u] = column(go, 16 + 4 * u, 32)
    ker_spec = dot(fwd_nat[...], jnp.concatenate([ker[...], ker[...]], axis=0))
    for j in range(0, 10, 2):
        lanes = slice(j * CH, (j + 2) * CH)
        s = dot(fwd[...], xw[:, lanes])
        spec[:, lanes] = s
        for i in range(2):
            parts[:, i * CH : (i + 1) * CH] = three_parts(cross(ker_spec, s[:, i * CH : (i + 1) * CH]))
        corr = dot(inv[...], parts[...])
        for i in range(2):
            mixed = (latf[j + i] + corr[:, i * CH : (i + 1) * CH]).astype(BF).astype(F4)
            latf[j + i] = mixed
            put_turned(m3, j + i, mixed, (-1, 0, 1))
    for j in range(0, 8, 4):
        v = b1[...]
        for q in range(3):
            v = v + dot(m3[j + q : j + q + 4].reshape(512, 384), w1[q])
        g = jax.nn.sigmoid(v)
        rise1[j * 128 : j * 128 + 512, :] = g * (1.0 + v * (1.0 - g))
        vg = v * g
        for i in range(4):
            h = (latf[j + i + 1] + vg[i * 128 : i * 128 + 128]).astype(BF).astype(F4)
            hid[j + i] = h
            put_turned(h3, j + i, h, (-2, 0, 2))
    v = b2[...]
    for q in range(3):
        v = v + dot(h3[2 * q : 2 * q + 4].reshape(512, 384), w2[q])
    g = jax.nn.sigmoid(v)
    p = hid[2:6].reshape(512, CH) + v * g
    for u in range(4):
        for rr in range(4):
            placed[pl.ds(u * 4 + rr, 32, stride=16), :] = p[u * 128 + rr * 32 : u * 128 + rr * 32 + 32]
    pred[...] = placed[...].astype(BF).reshape(PEERS, 16, CH)
    cot = cots[...].reshape(512, CH)
    own2 = (cot * (g * (1.0 + v * (1.0 - g)))).astype(BF)
    own2_wide = own2.astype(F4)
    for u in range(4):
        put_turned(s3, u, own2_wide[u * 128 : u * 128 + 128], (2, 0, -2))
    gh[...] = jnp.zeros(gh.shape, F4)
    gh[256:768, :] = cot
    for q in range(3):
        gh[q * 256 : q * 256 + 512, :] += dot(s3[...].reshape(512, 384), w2b[q])
    slope1 = (gh[...] * rise1[...]).astype(BF)
    slope1_wide = slope1.astype(F4)
    for u in range(8):
        put_turned(z3, u, slope1_wide[u * 128 : u * 128 + 128], (1, 0, -1))
    gm[...] = jnp.zeros(gm.shape, F4)
    gm[128:1152, :] = gh[...]
    for q in range(3):
        gm[q * 128 : q * 128 + 1024, :] += dot(z3[...].reshape(1024, 384), w1b[q])
    for q in range(3):
        d = dot_t(m3[q : q + 8].reshape(1024, 384), slope1)
        e = dot_t(h3[2 * q : 2 * q + 4].reshape(512, 384), own2)
        for p in range(3):
            at = (p * 3 + q) * 128
            halves[0, at : at + 128, :] = d[p * 128 : p * 128 + 128].astype(BF)
            halves[1, at : at + 128, :] = e[p * 128 : p * 128 + 128].astype(BF)
    both = jnp.zeros((N_ROWS, CH), F4)
    for j in range(0, 10, 2):
        two = jnp.concatenate([gm[(j + i) * 128 : (j + i) * 128 + 128, :] for i in range(2)], axis=1).astype(BF)
        s = dot(fwd[...], jnp.concatenate([two, two], axis=0))
        for i in range(2):
            both = both + cross(s[:, i * CH : (i + 1) * CH], spec[:, (j + i) * CH : (j + i + 1) * CH])
    halves[0, 1152:1280, :] = dot(inv_nat[...], three_parts(both)).astype(BF)
    rows = []
    for wide in (slope1_wide, own2_wide):
        b = jnp.sum(wide, axis=0, keepdims=True)
        high = b.astype(BF).astype(F4)
        rows += [high, b - high]
    tail = jnp.concatenate(rows + [jnp.zeros((124, CH), F4)], axis=0)
    halves[1, 1152:1280, :] = tail.astype(BF)
    core = lax.axis_index("c")
    keep[...] = halves[core]
    give[...] = halves[1 - core]


def finish_kernel(whole, dw1, dw2, dk, db1, db2):
    dw1[...] = whole[0:1152].astype(F4)
    dk[...] = whole[1152:1280].astype(F4)
    dw2[...] = whole[1280:2432].astype(F4)
    tail = whole[2432:2448].astype(F4)
    db1[...] = tail[0:1] + tail[1:2]
    db2[...] = tail[2:3] + tail[3:4]


def call(kernel, outs, scratch, flops, mib, *args):
    return pl.pallas_call(
        kernel,
        out_shape=[jax.ShapeDtypeStruct(s, d) for s, d in outs],
        in_specs=[VMEM] * len(args),
        out_specs=[VMEM] * len(outs),
        scratch_shapes=[pltpu.VMEM(s, d) for s, d in scratch],
        compiler_params=pltpu.CompilerParams(vmem_limit_bytes=mib << 20),
        cost_estimate=pl.CostEstimate(flops=flops, bytes_accessed=4 << 20, transcendentals=0),
    )(*args)


def local_step(left, own, right, ker, w1, b1, w2, b2):
    fwd, inv, fwd_nat, inv_nat = (jnp.asarray(t, BF) for t in tables())
    w1q, w2q = (w.transpose(1, 0, 2, 3).reshape(3, 384, CH) for w in (w1, w2))
    w1b, w2b = (w.transpose(1, 0, 3, 2).reshape(3, 384, CH) for w in (w1, w2))
    outs = [((PEERS, 16, CH), BF), ((1280, CH), BF), ((1280, CH), BF)]
    scratch = [((512, CH), F4), ((1024, CH), F4), ((512, CH), F4),
               ((10, 128, CH), F4), ((256, 10 * CH), BF), ((384, 2 * CH), BF), ((4, 128, CH), F4), ((8, 128, CH), F4),
               ((512, CH), F4), ((128, 10 * CH), F4), ((10, 128, 384), BF), ((8, 128, 384), BF), ((1024, CH), F4),
               ((4, 128, 384), BF), ((8, 128, 384), BF), ((1024, CH), F4), ((1280, CH), F4), ((2, 1280, CH), BF)]
    return call(step_kernel, outs, scratch, 3 << 30, 24, left, own, right, ker,
                w1q, b1.reshape(1, CH), w2q, b2.reshape(1, CH), w1b, w2b, fwd, inv, fwd_nat, inv_nat)


def sum_kernel(got, out):
    total = got[0].astype(F4)
    for i in range(1, got.shape[0]):
        total = total + got[i].astype(F4)
    total = total.astype(BF)
    for i in range(out.shape[0]):
        out[i] = total


def quarter_kernel(keep, got, mine, one, two, three, both):
    both[...] = (keep[...].astype(F4) + got[...].astype(F4)).astype(BF)
    x = lax.axis_index("x")
    for d, ref in enumerate((mine, one, two, three)):
        ref[...] = both[pl.ds(pl.multiple_of((x ^ d) * 320, 320), 320), :]


def add_kernel(mine, one, two, three, out):
    total = (mine[...].astype(F4) + one[...].astype(F4)) + (two[...].astype(F4) + three[...].astype(F4))
    out[...] = total.astype(BF)


def near_sums(keep, give):
    got = lax.ppermute(give, "c", [(0, 1), (1, 0)])
    mine, *given = call(quarter_kernel, [((320, CH), BF)] * 4, [((1280, CH), BF)], 1 << 20, 8, keep, got)
    got = [lax.ppermute(g, "x", [(x, x ^ d) for x in range(4)]) for d, g in enumerate(given, 1)]
    return call(add_kernel, [((320, CH), BF)], [], 1 << 20, 8, mine, *got)[0]


def summed(got, copies):
    (out,) = call(sum_kernel, [((copies,) + got.shape[1:], BF)], [], 1 << 20, 8, got)
    return out


def per_device(latent, corr_kernel, w1, b1, w2, b2, cotangent):
    row_count, col_count, _ = latent.shape
    flip = flipped(lax.axis_index("zh"), lax.axis_index("c"))
    block = pl.BlockSpec(latent.shape, lambda i: (0, 0, 0))
    send = pl.pallas_call(
        send_kernel,
        grid=(1,),
        out_shape=jax.ShapeDtypeStruct((PEERS, 32, CH), BF),
        in_specs=[block, block],
        out_specs=pl.BlockSpec((PEERS, 32, CH), lambda i: (0, 0, 0)),
        scratch_shapes=[pltpu.VMEM((1024, CH), F4), pltpu.VMEM((1024, CH), F4)],
        compiler_params=pltpu.CompilerParams(vmem_limit_bytes=60 << 20),
    )(latent, cotangent)
    own = lax.all_to_all(send, ROWS_AXES, 0, 0, tiled=True)
    ring = device_ring()
    n = len(ring)
    everywhere = ROWS_AXES + COLS_AXES

    def shifted(block, by):
        return lax.ppermute(block, everywhere, [(ring[i], ring[(i + by) % n]) for i in range(n)])

    left, right = shifted(own[:, 0:16], 1), shifted(own[:, 0:16], -1)
    pred_send, keep, give = local_step(left, own, right, corr_kernel, w1, b1, w2, b2)
    pred_got = lax.all_to_all(pred_send, ROWS_AXES, 0, 0, tiled=True)
    n_near, n_depth, n_plane = (lax.axis_size(axes) for axes in (NEAR_AXES, DEPTH_AXES, PLANE_AXES))
    part, pred_got = lax.optimization_barrier((near_sums(keep, give), pred_got))
    part = lax.all_to_all(part.reshape(n_near, 40, CH), NEAR_AXES, 0, 0, tiled=True)
    part = lax.all_to_all(summed(part, n_depth), DEPTH_AXES, 0, 0, tiled=True)
    whole = lax.all_to_all(summed(part, n_plane), PLANE_AXES, 0, 0, tiled=True).reshape(GRAD_ROWS, CH)

    got = pred_got.reshape(4, 8, 4, row_count, CH)
    even, odd = got[:, 0::2], got[::-1, 1::2]
    got = jnp.stack([even, odd], axis=2).reshape(4, 8, 4, row_count, CH).transpose(1, 0, 2, 3, 4)
    got = got.reshape(PEERS, 4, row_count, CH)
    got = jnp.where(flip, got[::-1], got)
    pred_out = got.transpose(2, 0, 1, 3).reshape(row_count, col_count, CH)

    shapes = [(1152, CH), (1152, CH), (CH, CH), (1, CH), (1, CH)]
    dw1, dw2, dk, db1, db2 = call(finish_kernel, [(shape, F4) for shape in shapes], [], 1 << 20, 8, whole)
    grad_shape = (3, 3, CH, CH)
    return pred_out, dw1.reshape(grad_shape), db1.reshape(CH), dw2.reshape(grad_shape), db2.reshape(CH), dk


def solution(mesh):
    split = Mesh(mesh.devices.reshape(tuple(SIZES[a] for a in ROWS_AXES + COLS_AXES)), ROWS_AXES + COLS_AXES)
    grid = P(ROWS_AXES, COLS_AXES, None)
    return jax.shard_map(
        per_device, mesh=split, in_specs=(grid, P(), P(), P(), P(), P(), grid),
        out_specs=(grid, P(), P(), P(), P(), P()), check_vma=False,
    )
```

```python
import jax
import jax.numpy as jnp
import numpy as np
from jax import lax
from jax.experimental import pallas as pl
from jax.experimental.pallas import tpu as pltpu
from jax.sharding import Mesh, PartitionSpec as P

ROWS_AXES = ("y", "zb", "za")
COLS_AXES = ("x", "zh", "c")
NEAR_AXES = ("x", "y", "za")
PLANE_AXES = ("c", "x", "y", "za")
DEPTH_AXES = ("zb", "zh")
SIZES = {"y": 4, "zb": 4, "za": 2, "x": 4, "zh": 2, "c": 2}
N_ROWS = 128
CH = 128
PEERS = 32
GRAD_ROWS = 2560
BF, F4 = jnp.bfloat16, jnp.float32
VMEM = pl.BlockSpec(memory_space=pltpu.VMEM)


def real_transform(order):
    freq = np.arange(64)
    angle = 2.0 * np.pi * ((freq[:, None] * order[None, :]) % N_ROWS) / N_ROWS
    sines = np.sin(angle)
    sines[0] = np.cos(np.pi * order)
    return np.concatenate([np.cos(angle), sines])


def split_two(table):
    high = table.astype(jnp.bfloat16)
    low = (table - high.astype(np.float64)).astype(jnp.bfloat16)
    return high, low


def tables():
    place = np.arange(N_ROWS)
    order = 4 * (place % 32) + place // 32
    weight = np.full((N_ROWS, 1), 2.0 / N_ROWS)
    weight[0] = weight[64] = 1.0 / N_ROWS
    made = []
    for rows in (order, place):
        made.append(np.concatenate(split_two(real_transform(rows)), axis=1))
        high, low = split_two((real_transform(rows) * weight).T)
        made.append(np.concatenate([high, high, low], axis=1))
    return made


def window_of(y, zl, flip):
    snake = zl * 4 + jnp.where(zl % 2 == 0, y, 3 - y)
    return jnp.where(flip, 31 - snake, snake)


def flipped(zh, c):
    return zh == c


def device_ring():
    ring = []
    for x in range(4):
        for zh in range(2):
            for c in range(2):
                block = [0] * 32
                for y in range(4):
                    for zl in range(8):
                        snake = zl * 4 + (y if zl % 2 == 0 else 3 - y)
                        block[31 - snake if flipped(zh, c) else snake] = (((y * 8 + zl) * 4 + x) * 2 + zh) * 2 + c
                ring += block
    return ring


def dot(a, b):
    return jnp.dot(a, b, preferred_element_type=F4)


def dot_t(a, b):
    return lax.dot_general(a, b, (((0,), (0,)), ((), ())), preferred_element_type=F4)


def turned(x, step):
    blocks = [x[32 * i : 32 * i + 32] for i in range(4)]
    if step > 0:
        moved = [pltpu.roll(b, 31, axis=0) for b in blocks[:step]]
        return jnp.concatenate(blocks[step:] + moved, axis=0)
    if step < 0:
        moved = [pltpu.roll(b, 1, axis=0) for b in blocks[step:]]
        return jnp.concatenate(moved + blocks[:step], axis=0)
    return x


def put_turned(ref, col, x, steps):
    for i, step in enumerate(steps):
        ref[col, :, i * CH : (i + 1) * CH] = turned(x, step).astype(BF)


def cross(first, second):
    fc, fs = first[:64], first[64:]
    sc, ss = second[:64], second[64:]
    real_row = lax.broadcasted_iota(jnp.int32, sc.shape, 0) == 0
    out_c = sc * fc + jnp.where(real_row, 0.0, ss * fs)
    out_s = jnp.where(real_row, ss * fs, ss * fc - sc * fs)
    return jnp.concatenate([out_c, out_s], axis=0)


def three_parts(x):
    high = x.astype(BF)
    low = (x - high.astype(F4)).astype(BF)
    return jnp.concatenate([high, low, high], axis=0)


def send_kernel(lat, cot, out, wide, packed):
    zh, c = lax.axis_index("zh"), lax.axis_index("c")
    flip = flipped(zh, c)
    for t, ref in enumerate((lat, cot)):
        wide[t * 512 : t * 512 + 512, :] = ref[...].reshape(512, CH).astype(F4)
    for k in range(PEERS):
        start = pl.multiple_of(4 * window_of(k // 8, jnp.int32(k % 8), flip), 4)
        for t in range(2):
            for rr in range(4):
                piece = wide[pl.ds(t * 512 + rr * 128 + start, 4), :]
                packed[pl.ds(k * 32 + t * 16 + rr, 4, stride=4), :] = piece
    out[...] = packed[...].astype(BF).reshape(PEERS, 32, CH)


def column(ref, start, stride):
    return jnp.concatenate([ref[pl.ds(start + rr, 32, stride=stride), :] for rr in range(4)], axis=0)


def step_kernel(left, own, right, ker, w1, b1, w2, b2, w1b, w2b, fwd, inv, fwd_nat, inv_nat,
                pred, keep, give,
                gl, go, gr, latf, xw, parts, cots, hid, placed, spec, m3, h3, rise1, s3, z3, gh, gm, halves):
    for ref, wide in ((left, gl), (own, go), (right, gr)):
        wide[...] = ref[...].reshape(wide.shape).astype(F4)
    lat_from = ([(gl, 4 * j, 16) for j in (1, 2, 3)] + [(go, 4 * j, 32) for j in range(4)]
                + [(gr, 4 * j, 16) for j in (0, 1, 2)])
    for j, (ref, start, stride) in enumerate(lat_from):
        x = column(ref, start, stride)
        latf[j] = x
        xb = x.astype(BF)
        xw[0:128, j * CH : (j + 1) * CH] = xb
        xw[128:256, j * CH : (j + 1) * CH] = xb
    for u in range(4):
        cots[u] = column(go, 16 + 4 * u, 32)
    ker_spec = dot(fwd_nat[...], jnp.concatenate([ker[...], ker[...]], axis=0))
    for j in range(0, 10, 2):
        lanes = slice(j * CH, (j + 2) * CH)
        s = dot(fwd[...], xw[:, lanes])
        spec[:, lanes] = s
        for i in range(2):
            parts[:, i * CH : (i + 1) * CH] = three_parts(cross(ker_spec, s[:, i * CH : (i + 1) * CH]))
        corr = dot(inv[...], parts[...])
        for i in range(2):
            mixed = (latf[j + i] + corr[:, i * CH : (i + 1) * CH]).astype(BF).astype(F4)
            latf[j + i] = mixed
            put_turned(m3, j + i, mixed, (-1, 0, 1))
    for j in range(0, 8, 4):
        v = b1[...]
        for q in range(3):
            v = v + dot(m3[j + q : j + q + 4].reshape(512, 384), w1[q])
        g = jax.nn.sigmoid(v)
        rise1[j * 128 : j * 128 + 512, :] = g * (1.0 + v * (1.0 - g))
        vg = v * g
        for i in range(4):
            h = (latf[j + i + 1] + vg[i * 128 : i * 128 + 128]).astype(BF).astype(F4)
            hid[j + i] = h
            put_turned(h3, j + i, h, (-2, 0, 2))
    v = b2[...]
    for q in range(3):
        v = v + dot(h3[2 * q : 2 * q + 4].reshape(512, 384), w2[q])
    g = jax.nn.sigmoid(v)
    p = hid[2:6].reshape(512, CH) + v * g
    for u in range(4):
        for rr in range(4):
            placed[pl.ds(u * 4 + rr, 32, stride=16), :] = p[u * 128 + rr * 32 : u * 128 + rr * 32 + 32]
    pred[...] = placed[...].astype(BF).reshape(PEERS, 16, CH)
    cot = cots[...].reshape(512, CH)
    own2 = (cot * (g * (1.0 + v * (1.0 - g)))).astype(BF)
    own2_wide = own2.astype(F4)
    for u in range(4):
        put_turned(s3, u, own2_wide[u * 128 : u * 128 + 128], (2, 0, -2))
    gh[...] = jnp.zeros(gh.shape, F4)
    gh[256:768, :] = cot
    for q in range(3):
        gh[q * 256 : q * 256 + 512, :] += dot(s3[...].reshape(512, 384), w2b[q])
    slope1 = (gh[...] * rise1[...]).astype(BF)
    slope1_wide = slope1.astype(F4)
    for u in range(8):
        put_turned(z3, u, slope1_wide[u * 128 : u * 128 + 128], (1, 0, -1))
    gm[...] = jnp.zeros(gm.shape, F4)
    gm[128:1152, :] = gh[...]
    for q in range(3):
        gm[q * 128 : q * 128 + 1024, :] += dot(z3[...].reshape(1024, 384), w1b[q])
    for q in range(3):
        d = dot_t(m3[q : q + 8].reshape(1024, 384), slope1)
        e = dot_t(h3[2 * q : 2 * q + 4].reshape(512, 384), own2)
        for p in range(3):
            at = (p * 3 + q) * 128
            halves[0, at : at + 128, :] = d[p * 128 : p * 128 + 128].astype(BF)
            halves[1, at : at + 128, :] = e[p * 128 : p * 128 + 128].astype(BF)
    both = jnp.zeros((N_ROWS, CH), F4)
    for j in range(0, 10, 2):
        two = jnp.concatenate([gm[(j + i) * 128 : (j + i) * 128 + 128, :] for i in range(2)], axis=1).astype(BF)
        s = dot(fwd[...], jnp.concatenate([two, two], axis=0))
        for i in range(2):
            both = both + cross(s[:, i * CH : (i + 1) * CH], spec[:, (j + i) * CH : (j + i + 1) * CH])
    halves[0, 1152:1280, :] = dot(inv_nat[...], three_parts(both)).astype(BF)
    rows = []
    for wide in (slope1_wide, own2_wide):
        b = jnp.sum(wide, axis=0, keepdims=True)
        high = b.astype(BF).astype(F4)
        rows += [high, b - high]
    tail = jnp.concatenate(rows + [jnp.zeros((124, CH), F4)], axis=0)
    halves[1, 1152:1280, :] = tail.astype(BF)
    core = lax.axis_index("c")
    keep[...] = halves[core]
    give[...] = halves[1 - core]


def finish_kernel(whole, dw1, dw2, dk, db1, db2):
    dw1[...] = whole[0:1152].astype(F4)
    dk[...] = whole[1152:1280].astype(F4)
    dw2[...] = whole[1280:2432].astype(F4)
    tail = whole[2432:2448].astype(F4)
    db1[...] = tail[0:1] + tail[1:2]
    db2[...] = tail[2:3] + tail[3:4]


def call(kernel, outs, scratch, flops, mib, *args):
    return pl.pallas_call(
        kernel,
        out_shape=[jax.ShapeDtypeStruct(s, d) for s, d in outs],
        in_specs=[VMEM] * len(args),
        out_specs=[VMEM] * len(outs),
        scratch_shapes=[pltpu.VMEM(s, d) for s, d in scratch],
        compiler_params=pltpu.CompilerParams(vmem_limit_bytes=mib << 20),
        cost_estimate=pl.CostEstimate(flops=flops, bytes_accessed=4 << 20, transcendentals=0),
    )(*args)


def local_step(left, own, right, ker, w1, b1, w2, b2):
    fwd, inv, fwd_nat, inv_nat = (jnp.asarray(t, BF) for t in tables())
    w1q, w2q = (w.transpose(1, 0, 2, 3).reshape(3, 384, CH) for w in (w1, w2))
    w1b, w2b = (w.transpose(1, 0, 3, 2).reshape(3, 384, CH) for w in (w1, w2))
    outs = [((PEERS, 16, CH), BF), ((1280, CH), BF), ((1280, CH), BF)]
    scratch = [((512, CH), F4), ((1024, CH), F4), ((512, CH), F4),
               ((10, 128, CH), F4), ((256, 10 * CH), BF), ((384, 2 * CH), BF), ((4, 128, CH), F4), ((8, 128, CH), F4),
               ((512, CH), F4), ((128, 10 * CH), F4), ((10, 128, 384), BF), ((8, 128, 384), BF), ((1024, CH), F4),
               ((4, 128, 384), BF), ((8, 128, 384), BF), ((1024, CH), F4), ((1280, CH), F4), ((2, 1280, CH), BF)]
    return call(step_kernel, outs, scratch, 3 << 30, 24, left, own, right, ker,
                w1q, b1.reshape(1, CH), w2q, b2.reshape(1, CH), w1b, w2b, fwd, inv, fwd_nat, inv_nat)


def sum_kernel(got, out):
    total = got[0].astype(F4)
    for i in range(1, got.shape[0]):
        total = total + got[i].astype(F4)
    total = total.astype(BF)
    for i in range(out.shape[0]):
        out[i] = total


def add_kernel(keep, got, out):
    out[...] = (keep[...].astype(F4) + got[...].astype(F4)).astype(BF)


def core_sum(keep, give):
    got = lax.ppermute(give, "c", [(0, 1), (1, 0)])
    return call(add_kernel, [((1280, CH), BF)], [], 1 << 20, 8, keep, got)[0]


def summed(got, copies):
    (out,) = call(sum_kernel, [((copies,) + got.shape[1:], BF)], [], 1 << 20, 8, got)
    return out


def per_device(latent, corr_kernel, w1, b1, w2, b2, cotangent):
    row_count, col_count, _ = latent.shape
    flip = flipped(lax.axis_index("zh"), lax.axis_index("c"))
    block = pl.BlockSpec(latent.shape, lambda i: (0, 0, 0))
    send = pl.pallas_call(
        send_kernel,
        grid=(1,),
        out_shape=jax.ShapeDtypeStruct((PEERS, 32, CH), BF),
        in_specs=[block, block],
        out_specs=pl.BlockSpec((PEERS, 32, CH), lambda i: (0, 0, 0)),
        scratch_shapes=[pltpu.VMEM((1024, CH), F4), pltpu.VMEM((1024, CH), F4)],
        compiler_params=pltpu.CompilerParams(vmem_limit_bytes=60 << 20),
    )(latent, cotangent)
    own = lax.all_to_all(send, ROWS_AXES, 0, 0, tiled=True)
    ring = device_ring()
    n = len(ring)
    everywhere = ROWS_AXES + COLS_AXES

    def shifted(block, by):
        return lax.ppermute(block, everywhere, [(ring[i], ring[(i + by) % n]) for i in range(n)])

    left, right = shifted(own[:, 0:16], 1), shifted(own[:, 0:16], -1)
    pred_send, keep, give = local_step(left, own, right, corr_kernel, w1, b1, w2, b2)
    pred_got = lax.all_to_all(pred_send, ROWS_AXES, 0, 0, tiled=True)
    n_near, n_depth, n_plane = (lax.axis_size(axes) for axes in (NEAR_AXES, DEPTH_AXES, PLANE_AXES))
    part, pred_got = lax.optimization_barrier((core_sum(keep, give), pred_got))
    part = lax.all_to_all(part.reshape(n_near, 40, CH), NEAR_AXES, 0, 0, tiled=True)
    part = lax.all_to_all(summed(part, n_depth), DEPTH_AXES, 0, 0, tiled=True)
    whole = lax.all_to_all(summed(part, n_plane), PLANE_AXES, 0, 0, tiled=True).reshape(GRAD_ROWS, CH)

    got = pred_got.reshape(4, 8, 4, row_count, CH)
    even, odd = got[:, 0::2], got[::-1, 1::2]
    got = jnp.stack([even, odd], axis=2).reshape(4, 8, 4, row_count, CH).transpose(1, 0, 2, 3, 4)
    got = got.reshape(PEERS, 4, row_count, CH)
    got = jnp.where(flip, got[::-1], got)
    pred_out = got.transpose(2, 0, 1, 3).reshape(row_count, col_count, CH)

    shapes = [(1152, CH), (1152, CH), (CH, CH), (1, CH), (1, CH)]
    dw1, dw2, dk, db1, db2 = call(finish_kernel, [(shape, F4) for shape in shapes], [], 1 << 20, 8, whole)
    grad_shape = (3, 3, CH, CH)
    return pred_out, dw1.reshape(grad_shape), db1.reshape(CH), dw2.reshape(grad_shape), db2.reshape(CH), dk


def solution(mesh):
    split = Mesh(mesh.devices.reshape(tuple(SIZES[a] for a in ROWS_AXES + COLS_AXES)), ROWS_AXES + COLS_AXES)
    grid = P(ROWS_AXES, COLS_AXES, None)
    return jax.shard_map(
        per_device, mesh=split, in_specs=(grid, P(), P(), P(), P(), P(), grid),
        out_specs=(grid, P(), P(), P(), P(), P()), check_vma=False,
    )
```

```python
import jax
import jax.numpy as jnp
import numpy as np
from jax import lax
from jax.experimental import pallas as pl
from jax.experimental.pallas import tpu as pltpu
from jax.sharding import Mesh, PartitionSpec as P

ROWS_AXES = ("y", "zb", "za")
COLS_AXES = ("x", "zh", "c")
NEAR_AXES = ("x", "y", "za")
PLANE_AXES = ("c", "x", "y", "za")
DEPTH_AXES = ("zb", "zh")
SIZES = {"y": 4, "zb": 4, "za": 2, "x": 4, "zh": 2, "c": 2}
N_ROWS = 128
CH = 128
PEERS = 32
GRAD_ROWS = 2560
BF, F4 = jnp.bfloat16, jnp.float32
VMEM = pl.BlockSpec(memory_space=pltpu.VMEM)


def real_transform(order):
    freq = np.arange(64)
    angle = 2.0 * np.pi * ((freq[:, None] * order[None, :]) % N_ROWS) / N_ROWS
    sines = np.sin(angle)
    sines[0] = np.cos(np.pi * order)
    return np.concatenate([np.cos(angle), sines])


def split_two(table):
    high = table.astype(jnp.bfloat16)
    low = (table - high.astype(np.float64)).astype(jnp.bfloat16)
    return high, low


def tables():
    place = np.arange(N_ROWS)
    order = 4 * (place % 32) + place // 32
    weight = np.full((N_ROWS, 1), 2.0 / N_ROWS)
    weight[0] = weight[64] = 1.0 / N_ROWS
    made = []
    for rows in (order, place):
        made.append(np.concatenate(split_two(real_transform(rows)), axis=1))
        high, low = split_two((real_transform(rows) * weight).T)
        made.append(np.concatenate([high, high, low], axis=1))
    return made


def window_of(y, zl, flip):
    snake = zl * 4 + jnp.where(zl % 2 == 0, y, 3 - y)
    return jnp.where(flip, 31 - snake, snake)


def flipped(zh, c):
    return zh == c


def device_ring():
    ring = []
    for x in range(4):
        for zh in range(2):
            for c in range(2):
                block = [0] * 32
                for y in range(4):
                    for zl in range(8):
                        snake = zl * 4 + (y if zl % 2 == 0 else 3 - y)
                        block[31 - snake if flipped(zh, c) else snake] = (((y * 8 + zl) * 4 + x) * 2 + zh) * 2 + c
                ring += block
    return ring


def dot(a, b):
    return jnp.dot(a, b, preferred_element_type=F4)


def dot_t(a, b):
    return lax.dot_general(a, b, (((0,), (0,)), ((), ())), preferred_element_type=F4)


def turned(x, step):
    blocks = [x[32 * i : 32 * i + 32] for i in range(4)]
    if step > 0:
        moved = [pltpu.roll(b, 31, axis=0) for b in blocks[:step]]
        return jnp.concatenate(blocks[step:] + moved, axis=0)
    if step < 0:
        moved = [pltpu.roll(b, 1, axis=0) for b in blocks[step:]]
        return jnp.concatenate(moved + blocks[:step], axis=0)
    return x


def put_turned(ref, col, x, steps):
    for i, step in enumerate(steps):
        ref[col, :, i * CH : (i + 1) * CH] = turned(x, step).astype(BF)


def cross(first, second):
    fc, fs = first[:64], first[64:]
    sc, ss = second[:64], second[64:]
    real_row = lax.broadcasted_iota(jnp.int32, sc.shape, 0) == 0
    out_c = sc * fc + jnp.where(real_row, 0.0, ss * fs)
    out_s = jnp.where(real_row, ss * fs, ss * fc - sc * fs)
    return jnp.concatenate([out_c, out_s], axis=0)


def three_parts(x):
    high = x.astype(BF)
    low = (x - high.astype(F4)).astype(BF)
    return jnp.concatenate([high, low, high], axis=0)


def send_kernel(lat, cot, out, staged, wide, packed, sems):
    zh, c = lax.axis_index("zh"), lax.axis_index("c")
    flip = flipped(zh, c)
    copies = [pltpu.make_async_copy(ref, staged.at[t], sems.at[t]) for t, ref in enumerate((lat, cot))]
    for copy in copies:
        copy.start()
    for t, copy in enumerate(copies):
        copy.wait()
        wide[t * 512 : t * 512 + 512, :] = staged[t].reshape(512, CH).astype(F4)
    for k in range(PEERS):
        start = pl.multiple_of(4 * window_of(k // 8, jnp.int32(k % 8), flip), 4)
        for t in range(2):
            for rr in range(4):
                piece = wide[pl.ds(t * 512 + rr * 128 + start, 4), :]
                packed[pl.ds(k * 32 + t * 16 + rr, 4, stride=4), :] = piece
    out[...] = packed[...].astype(BF).reshape(PEERS, 32, CH)


def column(ref, start, stride):
    return jnp.concatenate([ref[pl.ds(start + rr, 32, stride=stride), :] for rr in range(4)], axis=0)


def step_kernel(left, own, right, ker, w1, b1, w2, b2, w1b, w2b, fwd, inv, fwd_nat, inv_nat,
                pred, out,
                gl, go, gr, latf, xw, parts, cots, hid, placed, spec, m3, h3, rise1, s3, z3, gh, gm):
    for ref, wide in ((left, gl), (own, go), (right, gr)):
        wide[...] = ref[...].reshape(wide.shape).astype(F4)
    lat_from = ([(gl, 4 * j, 16) for j in (1, 2, 3)] + [(go, 4 * j, 32) for j in range(4)]
                + [(gr, 4 * j, 16) for j in (0, 1, 2)])
    for j, (ref, start, stride) in enumerate(lat_from):
        x = column(ref, start, stride)
        latf[j] = x
        xb = x.astype(BF)
        xw[0:128, j * CH : (j + 1) * CH] = xb
        xw[128:256, j * CH : (j + 1) * CH] = xb
    for u in range(4):
        cots[u] = column(go, 16 + 4 * u, 32)
    ker_spec = dot(fwd_nat[...], jnp.concatenate([ker[...], ker[...]], axis=0))
    for j in range(0, 10, 2):
        lanes = slice(j * CH, (j + 2) * CH)
        s = dot(fwd[...], xw[:, lanes])
        spec[:, lanes] = s
        for i in range(2):
            parts[:, i * CH : (i + 1) * CH] = three_parts(cross(ker_spec, s[:, i * CH : (i + 1) * CH]))
        corr = dot(inv[...], parts[...])
        for i in range(2):
            mixed = (latf[j + i] + corr[:, i * CH : (i + 1) * CH]).astype(BF).astype(F4)
            latf[j + i] = mixed
            put_turned(m3, j + i, mixed, (-1, 0, 1))
    for j in range(0, 8, 4):
        v = b1[...]
        for q in range(3):
            v = v + dot(m3[j + q : j + q + 4].reshape(512, 384), w1[q])
        g = jax.nn.sigmoid(v)
        rise1[j * 128 : j * 128 + 512, :] = g * (1.0 + v * (1.0 - g))
        vg = v * g
        for i in range(4):
            h = (latf[j + i + 1] + vg[i * 128 : i * 128 + 128]).astype(BF).astype(F4)
            hid[j + i] = h
            put_turned(h3, j + i, h, (-2, 0, 2))
    v = b2[...]
    for q in range(3):
        v = v + dot(h3[2 * q : 2 * q + 4].reshape(512, 384), w2[q])
    g = jax.nn.sigmoid(v)
    p = hid[2:6].reshape(512, CH) + v * g
    for u in range(4):
        for rr in range(4):
            placed[pl.ds(u * 4 + rr, 32, stride=16), :] = p[u * 128 + rr * 32 : u * 128 + rr * 32 + 32]
    pred[...] = placed[...].astype(BF).reshape(PEERS, 16, CH)
    cot = cots[...].reshape(512, CH)
    own2 = (cot * (g * (1.0 + v * (1.0 - g)))).astype(BF)
    own2_wide = own2.astype(F4)
    for u in range(4):
        put_turned(s3, u, own2_wide[u * 128 : u * 128 + 128], (2, 0, -2))
    gh[...] = jnp.zeros(gh.shape, F4)
    gh[256:768, :] = cot
    for q in range(3):
        gh[q * 256 : q * 256 + 512, :] += dot(s3[...].reshape(512, 384), w2b[q])
    slope1 = (gh[...] * rise1[...]).astype(BF)
    slope1_wide = slope1.astype(F4)
    for u in range(8):
        put_turned(z3, u, slope1_wide[u * 128 : u * 128 + 128], (1, 0, -1))
    gm[...] = jnp.zeros(gm.shape, F4)
    gm[128:1152, :] = gh[...]
    for q in range(3):
        gm[q * 128 : q * 128 + 1024, :] += dot(z3[...].reshape(1024, 384), w1b[q])
    for q in range(3):
        d = dot_t(m3[q : q + 8].reshape(1024, 384), slope1)
        e = dot_t(h3[2 * q : 2 * q + 4].reshape(512, 384), own2)
        for p in range(3):
            at = (p * 3 + q) * 128
            out[at : at + 128, :] = d[p * 128 : p * 128 + 128].astype(BF)
            out[1280 + at : 1408 + at, :] = e[p * 128 : p * 128 + 128].astype(BF)
    both = jnp.zeros((N_ROWS, CH), F4)
    for j in range(0, 10, 2):
        two = jnp.concatenate([gm[(j + i) * 128 : (j + i) * 128 + 128, :] for i in range(2)], axis=1).astype(BF)
        s = dot(fwd[...], jnp.concatenate([two, two], axis=0))
        for i in range(2):
            both = both + cross(s[:, i * CH : (i + 1) * CH], spec[:, (j + i) * CH : (j + i + 1) * CH])
    out[1152:1280, :] = dot(inv_nat[...], three_parts(both)).astype(BF)
    rows = []
    for wide in (slope1_wide, own2_wide):
        b = jnp.sum(wide, axis=0, keepdims=True)
        high = b.astype(BF).astype(F4)
        rows += [high, b - high]
    tail = jnp.concatenate(rows + [jnp.zeros((124, CH), F4)], axis=0)
    out[2432:2560, :] = tail.astype(BF)


def finish_kernel(whole, dw1, dw2, dk, db1, db2):
    dw1[...] = whole[0:1152].astype(F4)
    dk[...] = whole[1152:1280].astype(F4)
    dw2[...] = whole[1280:2432].astype(F4)
    tail = whole[2432:2448].astype(F4)
    db1[...] = tail[0:1] + tail[1:2]
    db2[...] = tail[2:3] + tail[3:4]


def call(kernel, outs, scratch, flops, mib, *args):
    return pl.pallas_call(
        kernel,
        out_shape=[jax.ShapeDtypeStruct(s, d) for s, d in outs],
        in_specs=[VMEM] * len(args),
        out_specs=[VMEM] * len(outs),
        scratch_shapes=[pltpu.VMEM(s, d) for s, d in scratch],
        compiler_params=pltpu.CompilerParams(vmem_limit_bytes=mib << 20),
        cost_estimate=pl.CostEstimate(flops=flops, bytes_accessed=4 << 20, transcendentals=0),
    )(*args)


def local_step(left, own, right, ker, w1, b1, w2, b2):
    fwd, inv, fwd_nat, inv_nat = (jnp.asarray(t, BF) for t in tables())
    w1q, w2q = (w.transpose(1, 0, 2, 3).reshape(3, 384, CH) for w in (w1, w2))
    w1b, w2b = (w.transpose(1, 0, 3, 2).reshape(3, 384, CH) for w in (w1, w2))
    outs = [((PEERS, 16, CH), BF), ((GRAD_ROWS, CH), BF)]
    scratch = [((512, CH), F4), ((1024, CH), F4), ((512, CH), F4),
               ((10, 128, CH), F4), ((256, 10 * CH), BF), ((384, 2 * CH), BF), ((4, 128, CH), F4), ((8, 128, CH), F4),
               ((512, CH), F4), ((128, 10 * CH), F4), ((10, 128, 384), BF), ((8, 128, 384), BF), ((1024, CH), F4),
               ((4, 128, 384), BF), ((8, 128, 384), BF), ((1024, CH), F4), ((1280, CH), F4)]
    return call(step_kernel, outs, scratch, 3 << 30, 24, left, own, right, ker,
                w1q, b1.reshape(1, CH), w2q, b2.reshape(1, CH), w1b, w2b, fwd, inv, fwd_nat, inv_nat)


def sum_kernel(got, out):
    total = got[0].astype(F4)
    for i in range(1, got.shape[0]):
        total = total + got[i].astype(F4)
    total = total.astype(BF)
    for i in range(out.shape[0]):
        out[i] = total


def half_kernel(grads, got, out):
    rows = pl.ds(pl.multiple_of(lax.axis_index("c") * 1280, 1280), 1280)
    out[...] = (grads[rows, :].astype(F4) + got[rows, :].astype(F4)).astype(BF)


def core_sum(grads):
    got = lax.ppermute(grads, "c", [(0, 1), (1, 0)])
    return call(half_kernel, [((GRAD_ROWS // 2, CH), BF)], [], 1 << 20, 8, grads, got)[0]


def summed(got, copies):
    (out,) = call(sum_kernel, [((copies,) + got.shape[1:], BF)], [], 1 << 20, 8, got)
    return out


def per_device(latent, corr_kernel, w1, b1, w2, b2, cotangent):
    row_count, col_count, _ = latent.shape
    flip = flipped(lax.axis_index("zh"), lax.axis_index("c"))
    send = pl.pallas_call(
        send_kernel,
        out_shape=jax.ShapeDtypeStruct((PEERS, 32, CH), BF),
        in_specs=[pl.BlockSpec(memory_space=pltpu.HBM)] * 2,
        out_specs=VMEM,
        scratch_shapes=[pltpu.VMEM((2, row_count, col_count, CH), BF), pltpu.VMEM((1024, CH), F4),
                        pltpu.VMEM((1024, CH), F4), pltpu.SemaphoreType.DMA((2,))],
        compiler_params=pltpu.CompilerParams(vmem_limit_bytes=8 << 20),
    )(*(pltpu.with_memory_space_constraint(a, pltpu.HBM) for a in (latent, cotangent)))
    own = lax.all_to_all(send, ROWS_AXES, 0, 0, tiled=True)
    ring = device_ring()
    n = len(ring)
    everywhere = ROWS_AXES + COLS_AXES

    def shifted(block, by):
        return lax.ppermute(block, everywhere, [(ring[i], ring[(i + by) % n]) for i in range(n)])

    left, right = shifted(own[:, 0:16], 1), shifted(own[:, 0:16], -1)
    pred_send, grads = local_step(left, own, right, corr_kernel, w1, b1, w2, b2)
    pred_got = lax.all_to_all(pred_send, ROWS_AXES, 0, 0, tiled=True)
    n_near, n_depth, n_plane = (lax.axis_size(axes) for axes in (NEAR_AXES, DEPTH_AXES, PLANE_AXES))
    part, pred_got = lax.optimization_barrier((core_sum(grads), pred_got))
    part = lax.all_to_all(part.reshape(n_near, 40, CH), NEAR_AXES, 0, 0, tiled=True)
    part = lax.all_to_all(summed(part, n_depth), DEPTH_AXES, 0, 0, tiled=True)
    whole = lax.all_to_all(summed(part, n_plane), PLANE_AXES, 0, 0, tiled=True).reshape(GRAD_ROWS, CH)

    got = pred_got.reshape(4, 8, 4, row_count, CH)
    even, odd = got[:, 0::2], got[::-1, 1::2]
    got = jnp.stack([even, odd], axis=2).reshape(4, 8, 4, row_count, CH).transpose(1, 0, 2, 3, 4)
    got = got.reshape(PEERS, 4, row_count, CH)
    got = jnp.where(flip, got[::-1], got)
    pred_out = got.transpose(2, 0, 1, 3).reshape(row_count, col_count, CH)

    shapes = [(1152, CH), (1152, CH), (CH, CH), (1, CH), (1, CH)]
    dw1, dw2, dk, db1, db2 = call(finish_kernel, [(shape, F4) for shape in shapes], [], 1 << 20, 8, whole)
    grad_shape = (3, 3, CH, CH)
    return pred_out, dw1.reshape(grad_shape), db1.reshape(CH), dw2.reshape(grad_shape), db2.reshape(CH), dk


def solution(mesh):
    split = Mesh(mesh.devices.reshape(tuple(SIZES[a] for a in ROWS_AXES + COLS_AXES)), ROWS_AXES + COLS_AXES)
    grid = P(ROWS_AXES, COLS_AXES, None)
    return jax.shard_map(
        per_device, mesh=split, in_specs=(grid, P(), P(), P(), P(), P(), grid),
        out_specs=(grid, P(), P(), P(), P(), P()), check_vma=False,
    )
```

```python
import jax
import jax.numpy as jnp
import numpy as np
from jax import lax
from jax.experimental import pallas as pl
from jax.experimental.pallas import tpu as pltpu
from jax.sharding import Mesh, PartitionSpec as P

ROWS_AXES = ("y", "zb", "za")
COLS_AXES = ("x", "zh", "c")
NEAR_AXES = ("x", "y", "za")
PLANE_AXES = ("c", "x", "y", "za")
DEPTH_AXES = ("zb", "zh")
SIZES = {"y": 4, "zb": 4, "za": 2, "x": 4, "zh": 2, "c": 2}
N_ROWS = 128
CH = 128
PEERS = 32
GRAD_ROWS = 2560
BF, F4 = jnp.bfloat16, jnp.float32
VMEM = pl.BlockSpec(memory_space=pltpu.VMEM)


def real_transform(order):
    freq = np.arange(64)
    angle = 2.0 * np.pi * ((freq[:, None] * order[None, :]) % N_ROWS) / N_ROWS
    sines = np.sin(angle)
    sines[0] = np.cos(np.pi * order)
    return np.concatenate([np.cos(angle), sines])


def split_two(table):
    high = table.astype(jnp.bfloat16)
    low = (table - high.astype(np.float64)).astype(jnp.bfloat16)
    return high, low


def tables():
    place = np.arange(N_ROWS)
    order = 4 * (place % 32) + place // 32
    weight = np.full((N_ROWS, 1), 2.0 / N_ROWS)
    weight[0] = weight[64] = 1.0 / N_ROWS
    made = []
    for rows in (order, place):
        made.append(np.concatenate(split_two(real_transform(rows)), axis=1))
        high, low = split_two((real_transform(rows) * weight).T)
        made.append(np.concatenate([high, high, low], axis=1))
    return made


def window_of(y, zl, flip):
    snake = zl * 4 + jnp.where(zl % 2 == 0, y, 3 - y)
    return jnp.where(flip, 31 - snake, snake)


def flipped(zh, c):
    return zh == c


def device_ring():
    ring = []
    for x in range(4):
        for zh in range(2):
            for c in range(2):
                block = [0] * 32
                for y in range(4):
                    for zl in range(8):
                        snake = zl * 4 + (y if zl % 2 == 0 else 3 - y)
                        block[31 - snake if flipped(zh, c) else snake] = (((y * 8 + zl) * 4 + x) * 2 + zh) * 2 + c
                ring += block
    return ring


def dot(a, b):
    return jnp.dot(a, b, preferred_element_type=F4)


def dot_t(a, b):
    return lax.dot_general(a, b, (((0,), (0,)), ((), ())), preferred_element_type=F4)


def turned(x, step):
    blocks = [x[32 * i : 32 * i + 32] for i in range(4)]
    if step > 0:
        moved = [pltpu.roll(b, 31, axis=0) for b in blocks[:step]]
        return jnp.concatenate(blocks[step:] + moved, axis=0)
    if step < 0:
        moved = [pltpu.roll(b, 1, axis=0) for b in blocks[step:]]
        return jnp.concatenate(moved + blocks[:step], axis=0)
    return x


def put_turned(ref, col, x, steps):
    for i, step in enumerate(steps):
        ref[col, :, i * CH : (i + 1) * CH] = turned(x, step).astype(BF)


def cross(first, second):
    fc, fs = first[:64], first[64:]
    sc, ss = second[:64], second[64:]
    real_row = lax.broadcasted_iota(jnp.int32, sc.shape, 0) == 0
    out_c = sc * fc + jnp.where(real_row, 0.0, ss * fs)
    out_s = jnp.where(real_row, ss * fs, ss * fc - sc * fs)
    return jnp.concatenate([out_c, out_s], axis=0)


def three_parts(x):
    high = x.astype(BF)
    low = (x - high.astype(F4)).astype(BF)
    return jnp.concatenate([high, low, high], axis=0)


def send_kernel(lat, cot, out, staged, wide, packed, sems):
    zh, c = lax.axis_index("zh"), lax.axis_index("c")
    flip = flipped(zh, c)
    copies = [pltpu.make_async_copy(ref, staged.at[t], sems.at[t]) for t, ref in enumerate((lat, cot))]
    for copy in copies:
        copy.start()
    for t, copy in enumerate(copies):
        copy.wait()
        wide[t * 512 : t * 512 + 512, :] = staged[t].reshape(512, CH).astype(F4)
    for k in range(PEERS):
        start = pl.multiple_of(4 * window_of(k // 8, jnp.int32(k % 8), flip), 4)
        for t in range(2):
            for rr in range(4):
                piece = wide[pl.ds(t * 512 + rr * 128 + start, 4), :]
                packed[pl.ds(k * 32 + t * 16 + rr, 4, stride=4), :] = piece
    out[...] = packed[...].astype(BF).reshape(PEERS, 32, CH)


def column(ref, start, stride):
    return jnp.concatenate([ref[pl.ds(start + rr, 32, stride=stride), :] for rr in range(4)], axis=0)


def step_kernel(left, own, right, ker, w1, b1, w2, b2, w1b, w2b, fwd, inv, fwd_nat, inv_nat,
                pred, keep, give,
                gl, go, gr, latf, xw, parts, cots, hid, placed, spec, m3, h3, rise1, s3, z3, gh, gm):
    for ref, wide in ((left, gl), (own, go), (right, gr)):
        wide[...] = ref[...].reshape(wide.shape).astype(F4)
    lat_from = ([(gl, 4 * j, 16) for j in (1, 2, 3)] + [(go, 4 * j, 32) for j in range(4)]
                + [(gr, 4 * j, 16) for j in (0, 1, 2)])
    for j, (ref, start, stride) in enumerate(lat_from):
        x = column(ref, start, stride)
        latf[j] = x
        xb = x.astype(BF)
        xw[0:128, j * CH : (j + 1) * CH] = xb
        xw[128:256, j * CH : (j + 1) * CH] = xb
    for u in range(4):
        cots[u] = column(go, 16 + 4 * u, 32)
    ker_spec = dot(fwd_nat[...], jnp.concatenate([ker[...], ker[...]], axis=0))
    for j in range(0, 10, 2):
        lanes = slice(j * CH, (j + 2) * CH)
        s = dot(fwd[...], xw[:, lanes])
        spec[:, lanes] = s
        for i in range(2):
            parts[:, i * CH : (i + 1) * CH] = three_parts(cross(ker_spec, s[:, i * CH : (i + 1) * CH]))
        corr = dot(inv[...], parts[...])
        for i in range(2):
            mixed = (latf[j + i] + corr[:, i * CH : (i + 1) * CH]).astype(BF).astype(F4)
            latf[j + i] = mixed
            put_turned(m3, j + i, mixed, (-1, 0, 1))
    for j in range(0, 8, 4):
        v = b1[...]
        for q in range(3):
            v = v + dot(m3[j + q : j + q + 4].reshape(512, 384), w1[q])
        g = jax.nn.sigmoid(v)
        rise1[j * 128 : j * 128 + 512, :] = g * (1.0 + v * (1.0 - g))
        vg = v * g
        for i in range(4):
            h = (latf[j + i + 1] + vg[i * 128 : i * 128 + 128]).astype(BF).astype(F4)
            hid[j + i] = h
            put_turned(h3, j + i, h, (-2, 0, 2))
    v = b2[...]
    for q in range(3):
        v = v + dot(h3[2 * q : 2 * q + 4].reshape(512, 384), w2[q])
    g = jax.nn.sigmoid(v)
    p = hid[2:6].reshape(512, CH) + v * g
    for u in range(4):
        for rr in range(4):
            placed[pl.ds(u * 4 + rr, 32, stride=16), :] = p[u * 128 + rr * 32 : u * 128 + rr * 32 + 32]
    pred[...] = placed[...].astype(BF).reshape(PEERS, 16, CH)
    cot = cots[...].reshape(512, CH)
    own2 = (cot * (g * (1.0 + v * (1.0 - g)))).astype(BF)
    own2_wide = own2.astype(F4)
    for u in range(4):
        put_turned(s3, u, own2_wide[u * 128 : u * 128 + 128], (2, 0, -2))
    gh[...] = jnp.zeros(gh.shape, F4)
    gh[256:768, :] = cot
    for q in range(3):
        gh[q * 256 : q * 256 + 512, :] += dot(s3[...].reshape(512, 384), w2b[q])
    slope1 = (gh[...] * rise1[...]).astype(BF)
    slope1_wide = slope1.astype(F4)
    for u in range(8):
        put_turned(z3, u, slope1_wide[u * 128 : u * 128 + 128], (1, 0, -1))
    gm[...] = jnp.zeros(gm.shape, F4)
    gm[128:1152, :] = gh[...]
    for q in range(3):
        gm[q * 128 : q * 128 + 1024, :] += dot(z3[...].reshape(1024, 384), w1b[q])
    def write(first, second):
        for q in range(3):
            d = dot_t(m3[q : q + 8].reshape(1024, 384), slope1)
            e = dot_t(h3[2 * q : 2 * q + 4].reshape(512, 384), own2)
            for p in range(3):
                at = (p * 3 + q) * 128
                first[at : at + 128, :] = d[p * 128 : p * 128 + 128].astype(BF)
                second[at : at + 128, :] = e[p * 128 : p * 128 + 128].astype(BF)
        both = jnp.zeros((N_ROWS, CH), F4)
        for j in range(0, 10, 2):
            two = jnp.concatenate([gm[(j + i) * 128 : (j + i) * 128 + 128, :] for i in range(2)], axis=1).astype(BF)
            s = dot(fwd[...], jnp.concatenate([two, two], axis=0))
            for i in range(2):
                both = both + cross(s[:, i * CH : (i + 1) * CH], spec[:, (j + i) * CH : (j + i + 1) * CH])
        first[1152:1280, :] = dot(inv_nat[...], three_parts(both)).astype(BF)
        rows = []
        for wide in (slope1_wide, own2_wide):
            b = jnp.sum(wide, axis=0, keepdims=True)
            high = b.astype(BF).astype(F4)
            rows += [high, b - high]
        tail = jnp.concatenate(rows + [jnp.zeros((124, CH), F4)], axis=0)
        second[1152:1280, :] = tail.astype(BF)

    core = lax.axis_index("c")
    pl.when(core == 0)(lambda: write(keep, give))
    pl.when(core == 1)(lambda: write(give, keep))


def finish_kernel(whole, dw1, dw2, dk, db1, db2):
    dw1[...] = whole[0:1152].astype(F4)
    dk[...] = whole[1152:1280].astype(F4)
    dw2[...] = whole[1280:2432].astype(F4)
    tail = whole[2432:2448].astype(F4)
    db1[...] = tail[0:1] + tail[1:2]
    db2[...] = tail[2:3] + tail[3:4]


def call(kernel, outs, scratch, flops, mib, *args):
    return pl.pallas_call(
        kernel,
        out_shape=[jax.ShapeDtypeStruct(s, d) for s, d in outs],
        in_specs=[VMEM] * len(args),
        out_specs=[VMEM] * len(outs),
        scratch_shapes=[pltpu.VMEM(s, d) for s, d in scratch],
        compiler_params=pltpu.CompilerParams(vmem_limit_bytes=mib << 20),
        cost_estimate=pl.CostEstimate(flops=flops, bytes_accessed=4 << 20, transcendentals=0),
    )(*args)


def local_step(left, own, right, ker, w1, b1, w2, b2):
    fwd, inv, fwd_nat, inv_nat = (jnp.asarray(t, BF) for t in tables())
    w1q, w2q = (w.transpose(1, 0, 2, 3).reshape(3, 384, CH) for w in (w1, w2))
    w1b, w2b = (w.transpose(1, 0, 3, 2).reshape(3, 384, CH) for w in (w1, w2))
    outs = [((PEERS, 16, CH), BF), ((GRAD_ROWS // 2, CH), BF), ((GRAD_ROWS // 2, CH), BF)]
    scratch = [((512, CH), F4), ((1024, CH), F4), ((512, CH), F4),
               ((10, 128, CH), F4), ((256, 10 * CH), BF), ((384, 2 * CH), BF), ((4, 128, CH), F4), ((8, 128, CH), F4),
               ((512, CH), F4), ((128, 10 * CH), F4), ((10, 128, 384), BF), ((8, 128, 384), BF), ((1024, CH), F4),
               ((4, 128, 384), BF), ((8, 128, 384), BF), ((1024, CH), F4), ((1280, CH), F4)]
    return call(step_kernel, outs, scratch, 3 << 30, 24, left, own, right, ker,
                w1q, b1.reshape(1, CH), w2q, b2.reshape(1, CH), w1b, w2b, fwd, inv, fwd_nat, inv_nat)


def sum_kernel(got, out):
    total = got[0].astype(F4)
    for i in range(1, got.shape[0]):
        total = total + got[i].astype(F4)
    total = total.astype(BF)
    for i in range(out.shape[0]):
        out[i] = total


def add_kernel(keep, got, out):
    out[...] = (keep[...].astype(F4) + got[...].astype(F4)).astype(BF)


def core_sum(keep, give):
    got = lax.ppermute(give, "c", [(0, 1), (1, 0)])
    return call(add_kernel, [((GRAD_ROWS // 2, CH), BF)], [], 1 << 20, 8, keep, got)[0]


def summed(got, copies):
    (out,) = call(sum_kernel, [((copies,) + got.shape[1:], BF)], [], 1 << 20, 8, got)
    return out


def per_device(latent, corr_kernel, w1, b1, w2, b2, cotangent):
    row_count, col_count, _ = latent.shape
    flip = flipped(lax.axis_index("zh"), lax.axis_index("c"))
    send = pl.pallas_call(
        send_kernel,
        out_shape=jax.ShapeDtypeStruct((PEERS, 32, CH), BF),
        in_specs=[pl.BlockSpec(memory_space=pltpu.HBM)] * 2,
        out_specs=VMEM,
        scratch_shapes=[pltpu.VMEM((2, row_count, col_count, CH), BF), pltpu.VMEM((1024, CH), F4),
                        pltpu.VMEM((1024, CH), F4), pltpu.SemaphoreType.DMA((2,))],
        compiler_params=pltpu.CompilerParams(vmem_limit_bytes=8 << 20),
    )(*(pltpu.with_memory_space_constraint(a, pltpu.HBM) for a in (latent, cotangent)))
    own = lax.all_to_all(send, ROWS_AXES, 0, 0, tiled=True)
    ring = device_ring()
    n = len(ring)
    everywhere = ROWS_AXES + COLS_AXES

    def shifted(block, by):
        return lax.ppermute(block, everywhere, [(ring[i], ring[(i + by) % n]) for i in range(n)])

    left, right = shifted(own[:, 0:16], 1), shifted(own[:, 0:16], -1)
    pred_send, keep, give = local_step(left, own, right, corr_kernel, w1, b1, w2, b2)
    pred_got = lax.all_to_all(pred_send, ROWS_AXES, 0, 0, tiled=True)
    n_near, n_depth, n_plane = (lax.axis_size(axes) for axes in (NEAR_AXES, DEPTH_AXES, PLANE_AXES))
    part, pred_got = lax.optimization_barrier((core_sum(keep, give), pred_got))
    part = lax.all_to_all(part.reshape(n_near, 40, CH), NEAR_AXES, 0, 0, tiled=True)
    part = lax.all_to_all(summed(part, n_depth), DEPTH_AXES, 0, 0, tiled=True)
    whole = lax.all_to_all(summed(part, n_plane), PLANE_AXES, 0, 0, tiled=True).reshape(GRAD_ROWS, CH)

    got = pred_got.reshape(4, 8, 4, row_count, CH)
    even, odd = got[:, 0::2], got[::-1, 1::2]
    got = jnp.stack([even, odd], axis=2).reshape(4, 8, 4, row_count, CH).transpose(1, 0, 2, 3, 4)
    got = got.reshape(PEERS, 4, row_count, CH)
    got = jnp.where(flip, got[::-1], got)
    pred_out = got.transpose(2, 0, 1, 3).reshape(row_count, col_count, CH)

    shapes = [(1152, CH), (1152, CH), (CH, CH), (1, CH), (1, CH)]
    dw1, dw2, dk, db1, db2 = call(finish_kernel, [(shape, F4) for shape in shapes], [], 1 << 20, 8, whole)
    grad_shape = (3, 3, CH, CH)
    return pred_out, dw1.reshape(grad_shape), db1.reshape(CH), dw2.reshape(grad_shape), db2.reshape(CH), dk


def solution(mesh):
    split = Mesh(mesh.devices.reshape(tuple(SIZES[a] for a in ROWS_AXES + COLS_AXES)), ROWS_AXES + COLS_AXES)
    grid = P(ROWS_AXES, COLS_AXES, None)
    return jax.shard_map(
        per_device, mesh=split, in_specs=(grid, P(), P(), P(), P(), P(), grid),
        out_specs=(grid, P(), P(), P(), P(), P()), check_vma=False,
    )
```

```python
import jax
import jax.numpy as jnp
import numpy as np
from jax import lax
from jax.experimental import pallas as pl
from jax.experimental.pallas import tpu as pltpu
from jax.sharding import Mesh, PartitionSpec as P

ROWS_AXES = ("y", "zb", "za")
COLS_AXES = ("x", "zh", "c")
NEAR_AXES = ("x", "y", "za")
PLANE_AXES = ("c", "x", "y", "za")
DEPTH_AXES = ("zb", "zh")
SIZES = {"y": 4, "zb": 4, "za": 2, "x": 4, "zh": 2, "c": 2}
N_ROWS = 128
CH = 128
PEERS = 32
GRAD_ROWS = 2560
BF, F4 = jnp.bfloat16, jnp.float32
VMEM = pl.BlockSpec(memory_space=pltpu.VMEM)


def real_transform(order):
    freq = np.arange(64)
    angle = 2.0 * np.pi * ((freq[:, None] * order[None, :]) % N_ROWS) / N_ROWS
    sines = np.sin(angle)
    sines[0] = np.cos(np.pi * order)
    return np.concatenate([np.cos(angle), sines])


def split_two(table):
    high = table.astype(jnp.bfloat16)
    low = (table - high.astype(np.float64)).astype(jnp.bfloat16)
    return high, low


def tables():
    place = np.arange(N_ROWS)
    order = 4 * (place % 32) + place // 32
    weight = np.full((N_ROWS, 1), 2.0 / N_ROWS)
    weight[0] = weight[64] = 1.0 / N_ROWS
    made = []
    for rows in (order, place):
        made.append(np.concatenate(split_two(real_transform(rows)), axis=1))
        high, low = split_two((real_transform(rows) * weight).T)
        made.append(np.concatenate([high, high, low], axis=1))
    return made


def window_of(y, zl, flip):
    snake = zl * 4 + jnp.where(zl % 2 == 0, y, 3 - y)
    return jnp.where(flip, 31 - snake, snake)


def flipped(zh, c):
    return zh == c


def device_ring():
    ring = []
    for x in range(4):
        for zh in range(2):
            for c in range(2):
                block = [0] * 32
                for y in range(4):
                    for zl in range(8):
                        snake = zl * 4 + (y if zl % 2 == 0 else 3 - y)
                        block[31 - snake if flipped(zh, c) else snake] = (((y * 8 + zl) * 4 + x) * 2 + zh) * 2 + c
                ring += block
    return ring


def dot(a, b):
    return jnp.dot(a, b, preferred_element_type=F4)


def dot_t(a, b):
    return lax.dot_general(a, b, (((0,), (0,)), ((), ())), preferred_element_type=F4)


def turned(x, step):
    blocks = [x[32 * i : 32 * i + 32] for i in range(4)]
    if step > 0:
        moved = [pltpu.roll(b, 31, axis=0) for b in blocks[:step]]
        return jnp.concatenate(blocks[step:] + moved, axis=0)
    if step < 0:
        moved = [pltpu.roll(b, 1, axis=0) for b in blocks[step:]]
        return jnp.concatenate(moved + blocks[:step], axis=0)
    return x


def put_turned(ref, col, x, steps):
    for i, step in enumerate(steps):
        ref[col, :, i * CH : (i + 1) * CH] = turned(x, step).astype(BF)


def cross(first, second):
    fc, fs = first[:64], first[64:]
    sc, ss = second[:64], second[64:]
    real_row = lax.broadcasted_iota(jnp.int32, sc.shape, 0) == 0
    out_c = sc * fc + jnp.where(real_row, 0.0, ss * fs)
    out_s = jnp.where(real_row, ss * fs, ss * fc - sc * fs)
    return jnp.concatenate([out_c, out_s], axis=0)


def three_parts(x):
    high = x.astype(BF)
    low = (x - high.astype(F4)).astype(BF)
    return jnp.concatenate([high, low, high], axis=0)


def send_kernel(lat, cot, out, staged, wide, packed, sems):
    zh, c = lax.axis_index("zh"), lax.axis_index("c")
    flip = flipped(zh, c)
    copies = [pltpu.make_async_copy(ref, staged.at[t], sems.at[t]) for t, ref in enumerate((lat, cot))]
    for copy in copies:
        copy.start()
    for t, copy in enumerate(copies):
        copy.wait()
        wide[t * 512 : t * 512 + 512, :] = staged[t].reshape(512, CH).astype(F4)
    for k in range(PEERS):
        start = pl.multiple_of(4 * window_of(k // 8, jnp.int32(k % 8), flip), 4)
        for t in range(2):
            for rr in range(4):
                piece = wide[pl.ds(t * 512 + rr * 128 + start, 4), :]
                packed[pl.ds(k * 32 + t * 16 + rr, 4, stride=4), :] = piece
    out[...] = packed[...].astype(BF).reshape(PEERS, 32, CH)


def column(ref, start, stride):
    return jnp.concatenate([ref[pl.ds(start + rr, 32, stride=stride), :] for rr in range(4)], axis=0)


def step_kernel(left, own, right, ker, w1, b1, w2, b2, w1b, w2b, fwd, inv, fwd_nat, inv_nat,
                pred, out,
                gl, go, gr, latf, xw, parts, cots, hid, placed, spec, m3, h3, rise1, s3, z3, gh, gm, biases, sems):
    copies = [pltpu.make_async_copy(b, biases.at[i], sems.at[i]) for i, b in enumerate((b1, b2))]
    for copy in copies:
        copy.start()
    for ref, wide in ((left, gl), (own, go), (right, gr)):
        wide[...] = ref[...].reshape(wide.shape).astype(F4)
    lat_from = ([(gl, 4 * j, 16) for j in (1, 2, 3)] + [(go, 4 * j, 32) for j in range(4)]
                + [(gr, 4 * j, 16) for j in (0, 1, 2)])
    for j, (ref, start, stride) in enumerate(lat_from):
        x = column(ref, start, stride)
        latf[j] = x
        xb = x.astype(BF)
        xw[0:128, j * CH : (j + 1) * CH] = xb
        xw[128:256, j * CH : (j + 1) * CH] = xb
    for u in range(4):
        cots[u] = column(go, 16 + 4 * u, 32)
    ker_spec = dot(fwd_nat[...], jnp.concatenate([ker[...], ker[...]], axis=0))
    for j in range(0, 10, 2):
        lanes = slice(j * CH, (j + 2) * CH)
        s = dot(fwd[...], xw[:, lanes])
        spec[:, lanes] = s
        for i in range(2):
            parts[:, i * CH : (i + 1) * CH] = three_parts(cross(ker_spec, s[:, i * CH : (i + 1) * CH]))
        corr = dot(inv[...], parts[...])
        for i in range(2):
            mixed = (latf[j + i] + corr[:, i * CH : (i + 1) * CH]).astype(BF).astype(F4)
            latf[j + i] = mixed
            put_turned(m3, j + i, mixed, (-1, 0, 1))
    for copy in copies:
        copy.wait()
    for j in range(0, 8, 4):
        v = biases[0]
        for q in range(3):
            v = v + dot(m3[j + q : j + q + 4].reshape(512, 384), w1[q])
        g = jax.nn.sigmoid(v)
        rise1[j * 128 : j * 128 + 512, :] = g * (1.0 + v * (1.0 - g))
        vg = v * g
        for i in range(4):
            h = (latf[j + i + 1] + vg[i * 128 : i * 128 + 128]).astype(BF).astype(F4)
            hid[j + i] = h
            put_turned(h3, j + i, h, (-2, 0, 2))
    v = biases[1]
    for q in range(3):
        v = v + dot(h3[2 * q : 2 * q + 4].reshape(512, 384), w2[q])
    g = jax.nn.sigmoid(v)
    p = hid[2:6].reshape(512, CH) + v * g
    for u in range(4):
        for rr in range(4):
            placed[pl.ds(u * 4 + rr, 32, stride=16), :] = p[u * 128 + rr * 32 : u * 128 + rr * 32 + 32]
    pred[...] = placed[...].astype(BF).reshape(PEERS, 16, CH)
    cot = cots[...].reshape(512, CH)
    own2 = (cot * (g * (1.0 + v * (1.0 - g)))).astype(BF)
    own2_wide = own2.astype(F4)
    for u in range(4):
        put_turned(s3, u, own2_wide[u * 128 : u * 128 + 128], (2, 0, -2))
    gh[...] = jnp.zeros(gh.shape, F4)
    gh[256:768, :] = cot
    for q in range(3):
        gh[q * 256 : q * 256 + 512, :] += dot(s3[...].reshape(512, 384), w2b[q])
    slope1 = (gh[...] * rise1[...]).astype(BF)
    slope1_wide = slope1.astype(F4)
    for u in range(8):
        put_turned(z3, u, slope1_wide[u * 128 : u * 128 + 128], (1, 0, -1))
    gm[...] = jnp.zeros(gm.shape, F4)
    gm[128:1152, :] = gh[...]
    for q in range(3):
        gm[q * 128 : q * 128 + 1024, :] += dot(z3[...].reshape(1024, 384), w1b[q])
    for q in range(3):
        d = dot_t(m3[q : q + 8].reshape(1024, 384), slope1)
        e = dot_t(h3[2 * q : 2 * q + 4].reshape(512, 384), own2)
        for p in range(3):
            at = (p * 3 + q) * 128
            out[at : at + 128, :] = d[p * 128 : p * 128 + 128].astype(BF)
            out[1280 + at : 1408 + at, :] = e[p * 128 : p * 128 + 128].astype(BF)
    both = jnp.zeros((N_ROWS, CH), F4)
    for j in range(0, 10, 2):
        two = jnp.concatenate([gm[(j + i) * 128 : (j + i) * 128 + 128, :] for i in range(2)], axis=1).astype(BF)
        s = dot(fwd[...], jnp.concatenate([two, two], axis=0))
        for i in range(2):
            both = both + cross(s[:, i * CH : (i + 1) * CH], spec[:, (j + i) * CH : (j + i + 1) * CH])
    out[1152:1280, :] = dot(inv_nat[...], three_parts(both)).astype(BF)
    rows = []
    for wide in (slope1_wide, own2_wide):
        b = jnp.sum(wide, axis=0, keepdims=True)
        high = b.astype(BF).astype(F4)
        rows += [high, b - high]
    tail = jnp.concatenate(rows + [jnp.zeros((124, CH), F4)], axis=0)
    out[2432:2560, :] = tail.astype(BF)


def finish_kernel(whole, dw1, dw2, dk, db1, db2):
    dw1[...] = whole[0:1152].astype(F4)
    dk[...] = whole[1152:1280].astype(F4)
    dw2[...] = whole[1280:2432].astype(F4)
    tail = whole[2432:2448].astype(F4)
    db1[...] = tail[0:1] + tail[1:2]
    db2[...] = tail[2:3] + tail[3:4]


def call(kernel, outs, scratch, flops, mib, *args, hbm=(), sems=0):
    return pl.pallas_call(
        kernel,
        out_shape=[jax.ShapeDtypeStruct(s, d) for s, d in outs],
        in_specs=[pl.BlockSpec(memory_space=pltpu.HBM) if i in hbm else VMEM for i in range(len(args))],
        out_specs=[VMEM] * len(outs),
        scratch_shapes=[pltpu.VMEM(s, d) for s, d in scratch] + [pltpu.SemaphoreType.DMA((sems,))] * (sems > 0),
        compiler_params=pltpu.CompilerParams(vmem_limit_bytes=mib << 20),
        cost_estimate=pl.CostEstimate(flops=flops, bytes_accessed=4 << 20, transcendentals=0),
    )(*args)


def local_step(left, own, right, ker, w1, b1, w2, b2):
    fwd, inv, fwd_nat, inv_nat = (jnp.asarray(t, BF) for t in tables())
    w1q, w2q = (w.transpose(1, 0, 2, 3).reshape(3, 384, CH) for w in (w1, w2))
    w1b, w2b = (w.transpose(1, 0, 3, 2).reshape(3, 384, CH) for w in (w1, w2))
    outs = [((PEERS, 16, CH), BF), ((GRAD_ROWS, CH), BF)]
    scratch = [((512, CH), F4), ((1024, CH), F4), ((512, CH), F4),
               ((10, 128, CH), F4), ((256, 10 * CH), BF), ((384, 2 * CH), BF), ((4, 128, CH), F4), ((8, 128, CH), F4),
               ((512, CH), F4), ((128, 10 * CH), F4), ((10, 128, 384), BF), ((8, 128, 384), BF), ((1024, CH), F4),
               ((4, 128, 384), BF), ((8, 128, 384), BF), ((1024, CH), F4), ((1280, CH), F4), ((2, 1, CH), F4)]
    b1, b2 = (pltpu.with_memory_space_constraint(b.reshape(1, CH), pltpu.HBM) for b in (b1, b2))
    return call(step_kernel, outs, scratch, 3 << 30, 24, left, own, right, ker,
                w1q, b1, w2q, b2, w1b, w2b, fwd, inv, fwd_nat, inv_nat, hbm=(5, 7), sems=2)


def sum_kernel(got, out):
    total = got[0].astype(F4)
    for i in range(1, got.shape[0]):
        total = total + got[i].astype(F4)
    total = total.astype(BF)
    for i in range(out.shape[0]):
        out[i] = total


def half_kernel(grads, got, out):
    rows = pl.ds(pl.multiple_of(lax.axis_index("c") * 1280, 1280), 1280)
    out[...] = (grads[rows, :].astype(F4) + got[...].astype(F4)).astype(BF)


def core_sum(grads):
    half = GRAD_ROWS // 2
    give = lax.dynamic_slice_in_dim(grads, (1 - lax.axis_index("c")) * half, half)
    got = lax.ppermute(give, "c", [(0, 1), (1, 0)])
    return call(half_kernel, [((half, CH), BF)], [], 1 << 20, 8, grads, got)[0]


def summed(got, copies):
    (out,) = call(sum_kernel, [((copies,) + got.shape[1:], BF)], [], 1 << 20, 8, got)
    return out


def per_device(latent, corr_kernel, w1, b1, w2, b2, cotangent):
    row_count, col_count, _ = latent.shape
    flip = flipped(lax.axis_index("zh"), lax.axis_index("c"))
    send = pl.pallas_call(
        send_kernel,
        out_shape=jax.ShapeDtypeStruct((PEERS, 32, CH), BF),
        in_specs=[pl.BlockSpec(memory_space=pltpu.HBM)] * 2,
        out_specs=VMEM,
        scratch_shapes=[pltpu.VMEM((2, row_count, col_count, CH), BF), pltpu.VMEM((1024, CH), F4),
                        pltpu.VMEM((1024, CH), F4), pltpu.SemaphoreType.DMA((2,))],
        compiler_params=pltpu.CompilerParams(vmem_limit_bytes=8 << 20),
    )(*(pltpu.with_memory_space_constraint(a, pltpu.HBM) for a in (latent, cotangent)))
    own = lax.all_to_all(send, ROWS_AXES, 0, 0, tiled=True)
    ring = device_ring()
    n = len(ring)
    everywhere = ROWS_AXES + COLS_AXES

    def shifted(block, by):
        return lax.ppermute(block, everywhere, [(ring[i], ring[(i + by) % n]) for i in range(n)])

    left, right = shifted(own[:, 0:16], 1), shifted(own[:, 0:16], -1)
    pred_send, grads = local_step(left, own, right, corr_kernel, w1, b1, w2, b2)
    pred_got = lax.all_to_all(pred_send, ROWS_AXES, 0, 0, tiled=True)
    n_near, n_depth, n_plane = (lax.axis_size(axes) for axes in (NEAR_AXES, DEPTH_AXES, PLANE_AXES))
    part, pred_got = lax.optimization_barrier((core_sum(grads), pred_got))
    part = lax.all_to_all(part.reshape(n_near, 40, CH), NEAR_AXES, 0, 0, tiled=True)
    part = lax.all_to_all(summed(part, n_depth), DEPTH_AXES, 0, 0, tiled=True)
    whole = lax.all_to_all(summed(part, n_plane), PLANE_AXES, 0, 0, tiled=True).reshape(GRAD_ROWS, CH)

    got = pred_got.reshape(4, 8, 4, row_count, CH)
    even, odd = got[:, 0::2], got[::-1, 1::2]
    got = jnp.stack([even, odd], axis=2).reshape(4, 8, 4, row_count, CH).transpose(1, 0, 2, 3, 4)
    got = got.reshape(PEERS, 4, row_count, CH)
    got = jnp.where(flip, got[::-1], got)
    pred_out = got.transpose(2, 0, 1, 3).reshape(row_count, col_count, CH)

    shapes = [(1152, CH), (1152, CH), (CH, CH), (1, CH), (1, CH)]
    dw1, dw2, dk, db1, db2 = call(finish_kernel, [(shape, F4) for shape in shapes], [], 1 << 20, 8, whole)
    grad_shape = (3, 3, CH, CH)
    return pred_out, dw1.reshape(grad_shape), db1.reshape(CH), dw2.reshape(grad_shape), db2.reshape(CH), dk


def solution(mesh):
    split = Mesh(mesh.devices.reshape(tuple(SIZES[a] for a in ROWS_AXES + COLS_AXES)), ROWS_AXES + COLS_AXES)
    grid = P(ROWS_AXES, COLS_AXES, None)
    return jax.shard_map(
        per_device, mesh=split, in_specs=(grid, P(), P(), P(), P(), P(), grid),
        out_specs=(grid, P(), P(), P(), P(), P()), check_vma=False,
    )
```

```python
import jax
import jax.numpy as jnp
import numpy as np
from jax import lax
from jax.experimental import pallas as pl
from jax.experimental.pallas import tpu as pltpu
from jax.sharding import Mesh, PartitionSpec as P

ROWS_AXES = ("y", "zb", "za")
COLS_AXES = ("x", "zh", "c")
NEAR_AXES = ("x", "y", "za")
PLANE_AXES = ("c", "x", "y", "za")
DEPTH_AXES = ("zb", "zh")
SIZES = {"y": 4, "zb": 4, "za": 2, "x": 4, "zh": 2, "c": 2}
N_ROWS = 128
CH = 128
PEERS = 32
GRAD_ROWS = 2560
BF, F4 = jnp.bfloat16, jnp.float32
VMEM = pl.BlockSpec(memory_space=pltpu.VMEM)


def real_transform(order):
    freq = np.arange(64)
    angle = 2.0 * np.pi * ((freq[:, None] * order[None, :]) % N_ROWS) / N_ROWS
    sines = np.sin(angle)
    sines[0] = np.cos(np.pi * order)
    return np.concatenate([np.cos(angle), sines])


def split_two(table):
    high = table.astype(jnp.bfloat16)
    low = (table - high.astype(np.float64)).astype(jnp.bfloat16)
    return high, low


def tables():
    place = np.arange(N_ROWS)
    order = 4 * (place % 32) + place // 32
    weight = np.full((N_ROWS, 1), 2.0 / N_ROWS)
    weight[0] = weight[64] = 1.0 / N_ROWS
    made = []
    for rows in (order, place):
        made.append(np.concatenate(split_two(real_transform(rows)), axis=1))
        high, low = split_two((real_transform(rows) * weight).T)
        made.append(np.concatenate([high, high, low], axis=1))
    return made


def window_of(y, zl, flip):
    snake = zl * 4 + jnp.where(zl % 2 == 0, y, 3 - y)
    return jnp.where(flip, 31 - snake, snake)


def flipped(zh, c):
    return zh == c


def device_ring():
    ring = []
    for x in range(4):
        for zh in range(2):
            for c in range(2):
                block = [0] * 32
                for y in range(4):
                    for zl in range(8):
                        snake = zl * 4 + (y if zl % 2 == 0 else 3 - y)
                        block[31 - snake if flipped(zh, c) else snake] = (((y * 8 + zl) * 4 + x) * 2 + zh) * 2 + c
                ring += block
    return ring


def dot(a, b):
    return jnp.dot(a, b, preferred_element_type=F4)


def dot_t(a, b):
    return lax.dot_general(a, b, (((0,), (0,)), ((), ())), preferred_element_type=F4)


def turned(x, step):
    blocks = [x[32 * i : 32 * i + 32] for i in range(4)]
    if step > 0:
        moved = [pltpu.roll(b, 31, axis=0) for b in blocks[:step]]
        return jnp.concatenate(blocks[step:] + moved, axis=0)
    if step < 0:
        moved = [pltpu.roll(b, 1, axis=0) for b in blocks[step:]]
        return jnp.concatenate(moved + blocks[:step], axis=0)
    return x


def put_turned(ref, col, x, steps):
    for i, step in enumerate(steps):
        ref[col, :, i * CH : (i + 1) * CH] = turned(x, step).astype(BF)


def cross(first, second):
    fc, fs = first[:64], first[64:]
    sc, ss = second[:64], second[64:]
    real_row = lax.broadcasted_iota(jnp.int32, sc.shape, 0) == 0
    out_c = sc * fc + jnp.where(real_row, 0.0, ss * fs)
    out_s = jnp.where(real_row, ss * fs, ss * fc - sc * fs)
    return jnp.concatenate([out_c, out_s], axis=0)


def three_parts(x):
    high = x.astype(BF)
    low = (x - high.astype(F4)).astype(BF)
    return jnp.concatenate([high, low, high], axis=0)


def send_kernel(lat, cot, out, staged, wide, packed, sems):
    zh, c = lax.axis_index("zh"), lax.axis_index("c")
    flip = flipped(zh, c)
    copies = [pltpu.make_async_copy(ref, staged.at[t], sems.at[t]) for t, ref in enumerate((lat, cot))]
    for copy in copies:
        copy.start()
    for t, copy in enumerate(copies):
        copy.wait()
        wide[t * 512 : t * 512 + 512, :] = staged[t].reshape(512, CH).astype(F4)
    for k in range(PEERS):
        start = pl.multiple_of(4 * window_of(k // 8, jnp.int32(k % 8), flip), 4)
        for t in range(2):
            for rr in range(4):
                piece = wide[pl.ds(t * 512 + rr * 128 + start, 4), :]
                packed[pl.ds(k * 32 + t * 16 + rr, 4, stride=4), :] = piece
    out[...] = packed[...].astype(BF).reshape(PEERS, 32, CH)


def column(ref, start, stride):
    return jnp.concatenate([ref[pl.ds(start + rr, 32, stride=stride), :] for rr in range(4)], axis=0)


def step_kernel(left, own, right, ker, biases, w1, w2, w1b, w2b, fwd, inv, fwd_nat, inv_nat,
                pred, out,
                gl, go, gr, latf, xw, parts, cots, hid, placed, spec, m3, h3, rise1, s3, z3, gh, gm):
    for ref, wide in ((left, gl), (own, go), (right, gr)):
        wide[...] = ref[...].reshape(wide.shape).astype(F4)
    lat_from = ([(gl, 4 * j, 16) for j in (1, 2, 3)] + [(go, 4 * j, 32) for j in range(4)]
                + [(gr, 4 * j, 16) for j in (0, 1, 2)])
    for j, (ref, start, stride) in enumerate(lat_from):
        x = column(ref, start, stride)
        latf[j] = x
        xb = x.astype(BF)
        xw[0:128, j * CH : (j + 1) * CH] = xb
        xw[128:256, j * CH : (j + 1) * CH] = xb
    for u in range(4):
        cots[u] = column(go, 16 + 4 * u, 32)
    ker_spec = dot(fwd_nat[...], jnp.concatenate([ker[...], ker[...]], axis=0))
    for j in range(0, 10, 2):
        lanes = slice(j * CH, (j + 2) * CH)
        s = dot(fwd[...], xw[:, lanes])
        spec[:, lanes] = s
        for i in range(2):
            parts[:, i * CH : (i + 1) * CH] = three_parts(cross(ker_spec, s[:, i * CH : (i + 1) * CH]))
        corr = dot(inv[...], parts[...])
        for i in range(2):
            mixed = (latf[j + i] + corr[:, i * CH : (i + 1) * CH]).astype(BF).astype(F4)
            latf[j + i] = mixed
            put_turned(m3, j + i, mixed, (-1, 0, 1))
    for j in range(0, 8, 4):
        v = biases[0:1, :]
        for q in range(3):
            v = v + dot(m3[j + q : j + q + 4].reshape(512, 384), w1[q])
        g = jax.nn.sigmoid(v)
        rise1[j * 128 : j * 128 + 512, :] = g * (1.0 + v * (1.0 - g))
        vg = v * g
        for i in range(4):
            h = (latf[j + i + 1] + vg[i * 128 : i * 128 + 128]).astype(BF).astype(F4)
            hid[j + i] = h
            put_turned(h3, j + i, h, (-2, 0, 2))
    v = biases[1:2, :]
    for q in range(3):
        v = v + dot(h3[2 * q : 2 * q + 4].reshape(512, 384), w2[q])
    g = jax.nn.sigmoid(v)
    p = hid[2:6].reshape(512, CH) + v * g
    for u in range(4):
        for rr in range(4):
            placed[pl.ds(u * 4 + rr, 32, stride=16), :] = p[u * 128 + rr * 32 : u * 128 + rr * 32 + 32]
    pred[...] = placed[...].astype(BF).reshape(PEERS, 16, CH)
    cot = cots[...].reshape(512, CH)
    own2 = (cot * (g * (1.0 + v * (1.0 - g)))).astype(BF)
    own2_wide = own2.astype(F4)
    for u in range(4):
        put_turned(s3, u, own2_wide[u * 128 : u * 128 + 128], (2, 0, -2))
    gh[...] = jnp.zeros(gh.shape, F4)
    gh[256:768, :] = cot
    for q in range(3):
        gh[q * 256 : q * 256 + 512, :] += dot(s3[...].reshape(512, 384), w2b[q])
    slope1 = (gh[...] * rise1[...]).astype(BF)
    slope1_wide = slope1.astype(F4)
    for u in range(8):
        put_turned(z3, u, slope1_wide[u * 128 : u * 128 + 128], (1, 0, -1))
    gm[...] = jnp.zeros(gm.shape, F4)
    gm[128:1152, :] = gh[...]
    for q in range(3):
        gm[q * 128 : q * 128 + 1024, :] += dot(z3[...].reshape(1024, 384), w1b[q])
    for q in range(3):
        d = dot_t(m3[q : q + 8].reshape(1024, 384), slope1)
        e = dot_t(h3[2 * q : 2 * q + 4].reshape(512, 384), own2)
        for p in range(3):
            at = (p * 3 + q) * 128
            out[at : at + 128, :] = d[p * 128 : p * 128 + 128].astype(BF)
            out[1280 + at : 1408 + at, :] = e[p * 128 : p * 128 + 128].astype(BF)
    both = jnp.zeros((N_ROWS, CH), F4)
    for j in range(0, 10, 2):
        two = jnp.concatenate([gm[(j + i) * 128 : (j + i) * 128 + 128, :] for i in range(2)], axis=1).astype(BF)
        s = dot(fwd[...], jnp.concatenate([two, two], axis=0))
        for i in range(2):
            both = both + cross(s[:, i * CH : (i + 1) * CH], spec[:, (j + i) * CH : (j + i + 1) * CH])
    out[1152:1280, :] = dot(inv_nat[...], three_parts(both)).astype(BF)
    rows = []
    for wide in (slope1_wide, own2_wide):
        b = jnp.sum(wide, axis=0, keepdims=True)
        high = b.astype(BF).astype(F4)
        rows += [high, b - high]
    tail = jnp.concatenate(rows + [jnp.zeros((124, CH), F4)], axis=0)
    out[2432:2560, :] = tail.astype(BF)


def finish_kernel(whole, dw1, dw2, dk, db1, db2):
    dw1[...] = whole[0:1152].astype(F4)
    dk[...] = whole[1152:1280].astype(F4)
    dw2[...] = whole[1280:2432].astype(F4)
    tail = whole[2432:2448].astype(F4)
    db1[...] = tail[0:1] + tail[1:2]
    db2[...] = tail[2:3] + tail[3:4]


def call(kernel, outs, scratch, flops, mib, *args):
    return pl.pallas_call(
        kernel,
        out_shape=[jax.ShapeDtypeStruct(s, d) for s, d in outs],
        in_specs=[VMEM] * len(args),
        out_specs=[VMEM] * len(outs),
        scratch_shapes=[pltpu.VMEM(s, d) for s, d in scratch],
        compiler_params=pltpu.CompilerParams(vmem_limit_bytes=mib << 20),
        cost_estimate=pl.CostEstimate(flops=flops, bytes_accessed=4 << 20, transcendentals=0),
    )(*args)


def local_step(left, own, right, ker, w1, b1, w2, b2):
    fwd, inv, fwd_nat, inv_nat = (jnp.asarray(t, BF) for t in tables())
    w1q, w2q = (w.transpose(1, 0, 2, 3).reshape(3, 384, CH) for w in (w1, w2))
    w1b, w2b = (w.transpose(1, 0, 3, 2).reshape(3, 384, CH) for w in (w1, w2))
    outs = [((PEERS, 16, CH), BF), ((GRAD_ROWS, CH), BF)]
    scratch = [((512, CH), F4), ((1024, CH), F4), ((512, CH), F4),
               ((10, 128, CH), F4), ((256, 10 * CH), BF), ((384, 2 * CH), BF), ((4, 128, CH), F4), ((8, 128, CH), F4),
               ((512, CH), F4), ((128, 10 * CH), F4), ((10, 128, 384), BF), ((8, 128, 384), BF), ((1024, CH), F4),
               ((4, 128, 384), BF), ((8, 128, 384), BF), ((1024, CH), F4), ((1280, CH), F4)]
    return call(step_kernel, outs, scratch, 3 << 30, 24, left, own, right, ker,
                jnp.stack([b1, b2]), w1q, w2q, w1b, w2b, fwd, inv, fwd_nat, inv_nat)


def sum_kernel(got, out):
    total = got[0].astype(F4)
    for i in range(1, got.shape[0]):
        total = total + got[i].astype(F4)
    total = total.astype(BF)
    for i in range(out.shape[0]):
        out[i] = total


def half_kernel(grads, got, out):
    rows = pl.ds(pl.multiple_of(lax.axis_index("c") * 1280, 1280), 1280)
    out[...] = (grads[rows, :].astype(F4) + got[...].astype(F4)).astype(BF)


def core_sum(grads):
    half = GRAD_ROWS // 2
    give = lax.dynamic_slice_in_dim(grads, (1 - lax.axis_index("c")) * half, half)
    got = lax.ppermute(give, "c", [(0, 1), (1, 0)])
    return call(half_kernel, [((half, CH), BF)], [], 1 << 20, 8, grads, got)[0]


def summed(got, copies):
    (out,) = call(sum_kernel, [((copies,) + got.shape[1:], BF)], [], 1 << 20, 8, got)
    return out


def per_device(latent, corr_kernel, w1, b1, w2, b2, cotangent):
    row_count, col_count, _ = latent.shape
    flip = flipped(lax.axis_index("zh"), lax.axis_index("c"))
    send = pl.pallas_call(
        send_kernel,
        out_shape=jax.ShapeDtypeStruct((PEERS, 32, CH), BF),
        in_specs=[pl.BlockSpec(memory_space=pltpu.HBM)] * 2,
        out_specs=VMEM,
        scratch_shapes=[pltpu.VMEM((2, row_count, col_count, CH), BF), pltpu.VMEM((1024, CH), F4),
                        pltpu.VMEM((1024, CH), F4), pltpu.SemaphoreType.DMA((2,))],
        compiler_params=pltpu.CompilerParams(vmem_limit_bytes=8 << 20),
    )(*(pltpu.with_memory_space_constraint(a, pltpu.HBM) for a in (latent, cotangent)))
    own = lax.all_to_all(send, ROWS_AXES, 0, 0, tiled=True)
    ring = device_ring()
    n = len(ring)
    everywhere = ROWS_AXES + COLS_AXES

    def shifted(block, by):
        return lax.ppermute(block, everywhere, [(ring[i], ring[(i + by) % n]) for i in range(n)])

    left, right = shifted(own[:, 0:16], 1), shifted(own[:, 0:16], -1)
    pred_send, grads = local_step(left, own, right, corr_kernel, w1, b1, w2, b2)
    pred_got = lax.all_to_all(pred_send, ROWS_AXES, 0, 0, tiled=True)
    n_near, n_depth, n_plane = (lax.axis_size(axes) for axes in (NEAR_AXES, DEPTH_AXES, PLANE_AXES))
    part, pred_got = lax.optimization_barrier((core_sum(grads), pred_got))
    part = lax.all_to_all(part.reshape(n_near, 40, CH), NEAR_AXES, 0, 0, tiled=True)
    part = lax.all_to_all(summed(part, n_depth), DEPTH_AXES, 0, 0, tiled=True)
    whole = lax.all_to_all(summed(part, n_plane), PLANE_AXES, 0, 0, tiled=True).reshape(GRAD_ROWS, CH)

    got = pred_got.reshape(4, 8, 4, row_count, CH)
    even, odd = got[:, 0::2], got[::-1, 1::2]
    got = jnp.stack([even, odd], axis=2).reshape(4, 8, 4, row_count, CH).transpose(1, 0, 2, 3, 4)
    got = got.reshape(PEERS, 4, row_count, CH)
    got = jnp.where(flip, got[::-1], got)
    pred_out = got.transpose(2, 0, 1, 3).reshape(row_count, col_count, CH)

    shapes = [(1152, CH), (1152, CH), (CH, CH), (1, CH), (1, CH)]
    dw1, dw2, dk, db1, db2 = call(finish_kernel, [(shape, F4) for shape in shapes], [], 1 << 20, 8, whole)
    grad_shape = (3, 3, CH, CH)
    return pred_out, dw1.reshape(grad_shape), db1.reshape(CH), dw2.reshape(grad_shape), db2.reshape(CH), dk


def solution(mesh):
    split = Mesh(mesh.devices.reshape(tuple(SIZES[a] for a in ROWS_AXES + COLS_AXES)), ROWS_AXES + COLS_AXES)
    grid = P(ROWS_AXES, COLS_AXES, None)
    return jax.shard_map(
        per_device, mesh=split, in_specs=(grid, P(), P(), P(), P(), P(), grid),
        out_specs=(grid, P(), P(), P(), P(), P()), check_vma=False,
    )
```
